32 devices in a mesh: dp: 8 (over y, x, core), fsdp: 4 (over z).
Axes of the slice: x: 2, y: 2, z: 4, core: 2. Of those that a mesh axis runs over, the one named last changes fastest.
Arguments:
- tokens: bfloat16 [64, 1024, 768], P('dp', 'fsdp'), may hold values from -6 to 6
- cotangent: bfloat16 [64, 1024, 768], P('dp', 'fsdp'), may hold values from -6 to 6
- lengths: int32 [8, 8], P('dp'), may hold values from 256 to 1024, as said below
- perm: int32 [8, 8], P('dp'), may hold values from 0 to 7, each once within a row
- ln1_gain: bfloat16 [768], P(('dp', 'fsdp')), may hold values from 0.5 to 1.5
- ln1_bias: bfloat16 [768], P(('dp', 'fsdp')), may hold values from -3 to 3
- w_qkv: bfloat16 [768, 2304], P(('dp', 'fsdp')), may hold values from -0.3125 to 0.3125
- w_out: bfloat16 [768, 768], P(('dp', 'fsdp')), may hold values from -2.5 to 2.5
- ln2_gain: bfloat16 [768], P(('dp', 'fsdp')), may hold values from 0.5 to 1.5
- ln2_bias: bfloat16 [768], P(('dp', 'fsdp')), may hold values from -3 to 3
- w_up: bfloat16 [768, 3072], P(('dp', 'fsdp')), may hold values from -0.21875 to 0.21875
- w_down: bfloat16 [3072, 768], P(('dp', 'fsdp')), may hold values from -0.75 to 0.75
Outputs:
- block_out: bfloat16 [64, 1024, 768], P('dp', 'fsdp')
- d_tokens: bfloat16 [64, 1024, 768], P('dp', 'fsdp')
- grad_ln1_gain: float32 [768], P(('dp', 'fsdp'))
- grad_ln1_bias: float32 [768], P(('dp', 'fsdp'))
- grad_w_qkv: float32 [768, 2304], P(('dp', 'fsdp'))
- grad_w_out: float32 [768, 768], P(('dp', 'fsdp'))
- grad_ln2_gain: float32 [768], P(('dp', 'fsdp'))
- grad_ln2_bias: float32 [768], P(('dp', 'fsdp'))
- grad_w_up: float32 [768, 3072], P(('dp', 'fsdp'))
- grad_w_down: float32 [3072, 768], P(('dp', 'fsdp'))
The draws below stay inside these ranges and needn't reach their ends.
Inputs may be any that keep to these rules, and one draw needn't show every extreme that they name: lengths[g, p] is the live length of sequence perm[g, p] of dp group g, dealt to fsdp index p // 2 as its micro-batch p % 2; each row holds 1024 and 256 at least once. `perm`: each row is a permutation of the group's 8 sequences.
All inputs are finite; a program needn't handle non-finite values.
Results may differ from the reference program's by a relative error of at most 0.014.
The reference program's roundings to bfloat16 on the way count: a program that leaves them out, or rounds other values in their place, can miss the bound.
Values may be sent and summed in bfloat16 or wider, within the bound.
No kernel may reach another device: no remote copies, remote signals or barrier semaphores. Data moves between devices by JAX's collectives and lax.ppermute only.
A program may use at most 384 MiB of HBM per device.

```python
import math
import jax
import jax.numpy as jnp
from jax import lax

D = 768
HEADS = 12
FF = 3072
DEPTH = 48
MB = 2
SEQ_MAX = 1024
MIN_LEN = 256
SEQS_G = 8
SEQS = 64
N_DP = 8


def draw_lengths(key, part):
    per_device = SEQS_G // MB
    group_rows = SEQS // SEQS_G
    drawn = jax.random.randint(key, (group_rows, SEQS_G), MIN_LEN, SEQ_MAX + 1).astype(jnp.int32)
    drawn = drawn.at[:, 0].set(SEQ_MAX).at[:, 1].set(MIN_LEN)
    ranked = -jnp.sort(-drawn, axis=1)
    rank_index = jnp.arange(SEQS_G, dtype=jnp.int32)
    round_index = rank_index // per_device
    position = rank_index % per_device
    device = jnp.where(round_index % 2 == 0, position, per_device - 1 - position)
    slot_index = device * MB + round_index
    return jnp.zeros((group_rows, SEQS_G), jnp.int32).at[:, slot_index].set(ranked)


def block_levels(own_key, dims, shards, least, top_value):
    level, own = 1.0, jax.random.fold_in(own_key, 6)
    for dim, blocks in shards:
        steps = jnp.exp(jax.random.uniform(jax.random.fold_in(own, dim), (blocks,), jnp.float32, least / len(shards), top_value / len(shards)))
        level = level * jnp.repeat(steps, dims[dim] // blocks).reshape([-1 if axis == dim else 1 for axis in range(len(dims))])
    return level


def bell_draw(own_key, extent, spread, reach, pieces=(), kind=jnp.bfloat16):
    values = jax.random.normal(own_key, extent, jnp.float32) * spread
    if len(pieces) > 0:
        values = block_levels(own_key, extent, pieces, -0.22, 0.18) * values
    return jnp.clip(values, min=-reach, max=reach).astype(kind)


def setup_inputs(seed: int = 0) -> dict:
    key_of = jax.random.split(jax.random.key(seed), 13)
    tokens = bell_draw(key_of[0], (SEQS, SEQ_MAX, D), 1.0, 6.0, ((0, 8), (1, 4)))
    cotangent = bell_draw(key_of[1], (SEQS, SEQ_MAX, D), 1.0, 6.0, ((0, 8), (1, 4)))
    lengths = draw_lengths(jax.random.fold_in(key_of[12], 71), 0)
    perm = jax.vmap(lambda own: jax.random.permutation(own, SEQS_G))(jax.random.split(key_of[3], N_DP)).reshape((N_DP, SEQS_G)).astype(jnp.int32)
    ln1_gain = jnp.clip(1.0 + 0.1 * jax.random.normal(key_of[4], (D,), jnp.float32), 0.5, 1.5).astype(jnp.bfloat16)
    ln1_bias = bell_draw(key_of[5], (D,), 0.5, 3.0, ((0, 32),))
    w_qkv = bell_draw(key_of[6], (D, 3 * D), (D // 2) ** -0.5, 0.3125, ((0, 32),))
    w_out = bell_draw(key_of[7], (D, D), 0.4, 2.5, ((0, 32),))
    ln2_gain = jnp.clip(1.0 + 0.1 * jax.random.normal(key_of[8], (D,), jnp.float32), 0.5, 1.5).astype(jnp.bfloat16)
    ln2_bias = bell_draw(key_of[9], (D,), 0.5, 3.0, ((0, 32),))
    w_up = bell_draw(key_of[10], (D, FF), D ** -0.5, 0.21875, ((0, 32),))
    w_down = bell_draw(key_of[11], (FF, D), (D // 12) ** -0.5, 0.75, ((0, 32),))
    return dict(tokens=tokens, cotangent=cotangent, lengths=lengths, perm=perm, ln1_gain=ln1_gain, ln1_bias=ln1_bias, w_qkv=w_qkv, w_out=w_out, ln2_gain=ln2_gain, ln2_bias=ln2_bias, w_up=w_up, w_down=w_down)


@jax.custom_vjp
def low(v):
    return lax.optimization_barrier(v.astype(jnp.bfloat16)).astype(jnp.float32)

@jax.custom_vjp
def low_back(v):
    return v

def low_keep(v):
    return (low(v), None)

def low_pass(kept, grad):
    return (grad,)

def back_keep(v):
    return (v, None)

def back_low(kept, grad):
    return (low(grad),)
low.defvjp(low_keep, low_pass)
low_back.defvjp(back_keep, back_low)
epsilon = 1e-05

def gelu_tanh(value):
    inner = 0.7978845608028654 * (value + 0.044715 * value * value * value)
    return 0.5 * value * (1.0 + jnp.tanh(inner))

def layer_norm(seq_rows, gain, bias):
    center = seq_rows - lax.optimization_barrier(jnp.mean(seq_rows, axis=-1, keepdims=True))
    factor = lax.rsqrt(lax.optimization_barrier(jnp.mean(center * center, axis=-1, keepdims=True)) + epsilon)
    return center * factor * gain + bias

def product(left, right):
    return jnp.dot(left, right, preferred_element_type=jnp.float32, precision=lax.Precision.HIGHEST)

def one_sequence(params, seq_rows, length):
    gain_one, bias_one, w_qkv, w_out, gain_two, bias_two, w_up, w_down = params
    row_count = seq_rows.shape[0]
    model_width = seq_rows.shape[1]
    head_size = model_width // HEADS
    branch = 1.0 / math.sqrt(DEPTH)
    first_low = low(layer_norm(seq_rows, gain_one, bias_one))
    qkv_low = low(low_back(product(first_low, w_qkv)))
    queries = qkv_low[:, :model_width].reshape(row_count, HEADS, head_size)
    key_rows = qkv_low[:, model_width:2 * model_width].reshape(row_count, HEADS, head_size)
    values = qkv_low[:, 2 * model_width:].reshape(row_count, HEADS, head_size)
    scores = jnp.einsum('qhd,khd->hqk', queries, key_rows, precision=lax.Precision.HIGHEST, preferred_element_type=jnp.float32) * (1.0 / math.sqrt(head_size))
    scores = low_back(scores)
    places = lax.iota(jnp.int32, row_count)
    allowed = (places[None, :] <= places[:, None]) & (places[None, :] < length)
    scores = jnp.where(allowed[None], scores, -1e+30)
    row_peak = lax.optimization_barrier(jnp.max(scores, axis=-1, keepdims=True))
    exponent = jnp.exp(scores - row_peak)
    attn_probs = exponent / lax.optimization_barrier(jnp.sum(exponent, axis=-1, keepdims=True))
    mixed_rows = jnp.einsum('hqk,khd->qhd', low(attn_probs), values, precision=lax.Precision.HIGHEST, preferred_element_type=jnp.float32).reshape(row_count, model_width)
    attn_low = low(low_back(mixed_rows))
    middle = seq_rows + branch * low_back(product(attn_low, w_out))
    second_low = low(layer_norm(middle, gain_two, bias_two))
    up_proj = low_back(product(second_low, w_up))
    gelu_low = low(gelu_tanh(up_proj))
    final_rows = middle + branch * low_back(product(gelu_low, w_down))
    return jnp.where((places < length)[:, None], final_rows, 0.0)

def reference(tokens, cotangent, lengths, perm, ln1_gain, ln1_bias, w_qkv, w_out, ln2_gain, ln2_bias, w_up, w_down):
    group_count = perm.shape[0]
    slot_index = (lax.iota(jnp.int32, group_count)[:, None] * SEQS_G + perm.astype(jnp.int32)).reshape(-1)
    given_lengths = jnp.zeros((group_count * SEQS_G,), jnp.int32).at[slot_index].set(lengths.reshape(-1).astype(jnp.int32))
    params = tuple((piece.astype(jnp.float32) for piece in (ln1_gain, ln1_bias, w_qkv, w_out, ln2_gain, ln2_bias, w_up, w_down)))
    single = jax.checkpoint(one_sequence)

    def forward(weights, all_rows):
        return lax.map(lambda seq_item: single(weights, seq_item[0], seq_item[1]), (all_rows, given_lengths))
    result, pullback = jax.vjp(forward, params, tokens.astype(jnp.float32))
    weight_grads, grad_tokens = pullback(cotangent.astype(jnp.float32))
    return (result.astype(jnp.bfloat16), grad_tokens.astype(jnp.bfloat16), weight_grads[0], weight_grads[1], weight_grads[2], weight_grads[3], weight_grads[4], weight_grads[5], weight_grads[6], weight_grads[7])
```

```python
import math

import jax
import jax.numpy as jnp
from jax import lax
from jax.experimental import pallas as pl
from jax.experimental.pallas import tpu as pltpu
from jax.sharding import PartitionSpec as P

HEADS = 12
DEPTH = 48
EPS = 1e-05
ROWS = 256
BF = jnp.bfloat16
F32 = jnp.float32
ALPHA = 1.0 / math.sqrt(DEPTH)
GELU_C = 0.7978845608028654
GELU_A = 0.044715
VMEM_LIMIT = 60 * 1024 * 1024


def dot(a, b, ca=1, cb=0):
    return lax.dot_general(a, b, (((ca,), (cb,)), ((), ())), preferred_element_type=F32)


def norm(v):
    c = v - jnp.mean(v, axis=-1, keepdims=True)
    r = lax.rsqrt(jnp.mean(c * c, axis=-1, keepdims=True) + EPS)
    return c * r, r


def norm_back(f, n, r):
    return r * (f - jnp.mean(f, axis=-1, keepdims=True) - n * jnp.mean(f * n, axis=-1, keepdims=True))


def params(n):
    return pltpu.CompilerParams(
        dimension_semantics=("arbitrary",) * n, vmem_limit_bytes=VMEM_LIMIT
    )


def last_block(lens, m):
    return (lens[m] + (ROWS - 1)) // ROWS - 1


def lane_half(shape):
    return lax.broadcasted_iota(jnp.int32, shape, len(shape) - 1) < 64


def attn_fwd_kernel(lens, x_ref, w_ref, vec_ref, qkv_ref, low_ref, lse_ref, kv_ref, col_ref):
    m = pl.program_id(0)
    i = pl.program_id(1)
    d = x_ref.shape[2]
    blocks = pl.num_programs(1)
    live = i <= last_block(lens, m)

    @pl.when(live)
    def _():
        n, _ = norm(x_ref[0].astype(F32))
        low = (n * vec_ref[0:1, :] + vec_ref[1:2, :]).astype(BF)
        for t in range(3):
            part = dot(low, w_ref[:, t * d:(t + 1) * d]).astype(BF)
            qkv_ref[0, :, t * d:(t + 1) * d] = part
            if t:
                kv_ref[pl.ds(pl.multiple_of(i * ROWS, ROWS), ROWS), (t - 1) * d:t * d] = part
        col_ref[...] = jnp.zeros_like(col_ref)

    lane = lax.broadcasted_iota(jnp.int32, (ROWS, 128), 1)
    row = lax.broadcasted_iota(jnp.int32, (ROWS, ROWS), 0)
    key = lax.broadcasted_iota(jnp.int32, (ROWS, ROWS), 1)

    def variant(ii):
        keys = (ii + 1) * ROWS

        @pl.when(live & (i == ii))
        def _():
            allowed = (key <= row) & (key + ii * ROWS < lens[m])

            def pair(hp, carry):
                at = pl.multiple_of(hp * 128, 128)
                q = qkv_ref[0, :, pl.ds(at, 128)].astype(F32) * 0.125
                k = kv_ref[0:keys, pl.ds(at, 128)]
                v = kv_ref[0:keys, pl.ds(pl.multiple_of(d + at, 128), 128)]
                outs = []
                cols = col_ref[...]
                for h in range(2):
                    qh = jnp.where((lane < 64) == (h == 0), q, 0.0).astype(BF)
                    s = dot(qh, k, 1, 1)
                    tail = jnp.where(allowed, s[:, ii * ROWS:], -1e30)
                    s = tail if ii == 0 else jnp.concatenate([s[:, :ii * ROWS], tail], axis=1)
                    peak = jnp.max(s, axis=-1, keepdims=True)
                    e = jnp.exp(s - peak)
                    total = jnp.sum(e, axis=-1, keepdims=True)
                    p = (e * (1.0 / total)).astype(BF)
                    outs.append(dot(p, v))
                    cols = jnp.where(lane == hp * 2 + h, peak + jnp.log(total), cols)
                low_ref[0, :, pl.ds(at, 128)] = jnp.where(lane < 64, outs[0], outs[1]).astype(BF)
                col_ref[...] = cols
                return carry

            lax.fori_loop(0, d // 128, pair, 0)
            lse_ref[0] = jnp.transpose(col_ref[...])[0:16]

    for ii in range(x_rows_blocks(kv_ref)):
        variant(ii)


def x_rows_blocks(ref):
    return ref.shape[0] // ROWS


def attn_fwd(lens, x, w, vec):
    mb, rows, d = x.shape
    nb = rows // ROWS

    def blk(m, i, ln):
        return (m, jnp.minimum(i, last_block(ln, m)), 0)

    return pl.pallas_call(
        attn_fwd_kernel,
        grid_spec=pltpu.PrefetchScalarGridSpec(
            num_scalar_prefetch=1,
            grid=(mb, nb),
            in_specs=[
                pl.BlockSpec((1, ROWS, d), blk),
                pl.BlockSpec((d, 3 * d), lambda m, i, ln: (0, 0), pipeline_mode=pl.Buffered(1)),
                pl.BlockSpec((8, d), lambda m, i, ln: (0, 0)),
            ],
            out_specs=[
                pl.BlockSpec((1, ROWS, 3 * d), blk),
                pl.BlockSpec((1, ROWS, d), blk),
                pl.BlockSpec((1, 16, ROWS), lambda m, i, ln: (m, 0, jnp.minimum(i, last_block(ln, m)))),
            ],
            scratch_shapes=[pltpu.VMEM((rows, 2 * d), BF), pltpu.VMEM((ROWS, 128), F32)],
        ),
        out_shape=[
            jax.ShapeDtypeStruct((mb, rows, 3 * d), BF),
            jax.ShapeDtypeStruct((mb, rows, d), BF),
            jax.ShapeDtypeStruct((mb, 16, rows), F32),
        ],
        compiler_params=params(2),
        name="attn_fwd",
    )(lens, x, w, vec)


def mlp_kernel(lens, low_ref, x_ref, cot_ref, wout_ref, wup_ref, wdown_ref, vec_ref,
               out_ref, gmid_ref, gmix_ref, inner_ref, gmain_ref, gdown_ref, gvec_ref,
               aout_ref, aup_ref, adown_ref, stage_ref, sem):
    m = pl.program_id(0)
    i = pl.program_id(1)
    d = x_ref.shape[2]
    ff = wup_ref.shape[1]
    chunks = ff // d
    live = i <= last_block(lens, m)
    first = (m == 0) & (i == 0)
    final = (m == pl.num_programs(0) - 1) & (i == pl.num_programs(1) - 1)

    @pl.when(first)
    def _():
        aout_ref[...] = jnp.zeros_like(aout_ref)
        aup_ref[...] = jnp.zeros_like(aup_ref)
        adown_ref[...] = jnp.zeros_like(adown_ref)
        gvec_ref[...] = jnp.zeros_like(gvec_ref)

    @pl.when(jnp.logical_not(live))
    def _():
        out_ref[...] = jnp.zeros_like(out_ref)

    @pl.when(live)
    def _():
        alive = lax.broadcasted_iota(jnp.int32, (ROWS, 1), 0) + i * ROWS < lens[m]
        low = low_ref[0]
        middle = x_ref[0].astype(F32) + ALPHA * dot(low, wout_ref[...])
        n2, r2 = norm(middle)
        gain = vec_ref[2:3, :]
        second = (n2 * gain + vec_ref[3:4, :]).astype(BF)
        second_t = jnp.transpose(second)
        gout = jnp.where(alive, cot_ref[0].astype(F32), 0.0)
        gmlp = (ALPHA * gout).astype(BF)
        y = jnp.zeros((ROWS, d), F32)
        e2 = jnp.zeros((ROWS, d), F32)
        for c in range(chunks):
            at = slice(c * d, (c + 1) * d)
            up = dot(second, wup_ref[:, at])
            sq = up * up
            t = jnp.tanh(GELU_C * (up + GELU_A * sq * up))
            half = 0.5 * (1.0 + t)
            act = (up * half).astype(BF)
            slope = half + 0.5 * up * (1.0 - t * t) * (GELU_C * (1.0 + 3.0 * GELU_A * sq))
            gup = (dot(gmlp, wdown_ref[at, :], 1, 1) * slope).astype(BF)
            y = y + dot(act, wdown_ref[at, :])
            e2 = e2 + dot(gup, wup_ref[:, at], 1, 1)
            aup_ref[:, at] += dot(second_t, gup)
            adown_ref[at, :] += dot(act, gmlp, 0, 0)
        out_ref[0] = jnp.where(alive, middle + ALPHA * y, 0.0).astype(BF)
        gvec_ref[0:1, :] += jnp.sum(e2 * n2, axis=0, keepdims=True)
        gvec_ref[1:2, :] += jnp.sum(e2, axis=0, keepdims=True)
        gmid = gout + norm_back(e2 * gain, n2, r2)
        gmid_ref[0] = gmid
        gao = (ALPHA * gmid).astype(BF)
        aout_ref[...] += dot(low, gao, 0, 0)
        gmix = dot(gao, wout_ref[...], 1, 1).astype(BF)
        gmix_ref[0] = gmix
        prod = gmix.astype(F32) * low.astype(F32)
        head = lax.broadcasted_iota(jnp.int32, (16, d), 0)
        lane = lax.broadcasted_iota(jnp.int32, (16, d), 1)
        pick = jnp.where(lane // 64 == head, 1.0, 0.0).astype(F32)
        inner_ref[0] = lax.dot_general(
            pick, prod, (((1,), (1,)), ((), ())),
            preferred_element_type=F32, precision=lax.Precision.HIGHEST,
        )

    @pl.when(final)
    def _():
        stage_ref[:, 0:d] = aout_ref[...].astype(BF)
        stage_ref[:, d:] = aup_ref[...].astype(BF)
        main = pltpu.make_async_copy(stage_ref, gmain_ref, sem.at[0])
        main.start()
        main.wait()
        for c in range(chunks):
            stage_ref[:, c * d:(c + 1) * d] = adown_ref[c * d:(c + 1) * d, :].astype(BF)
        copies = []
        for c in range(chunks):
            copies.append(pltpu.make_async_copy(
                stage_ref.at[:, c * d:(c + 1) * d], gdown_ref.at[c * d:(c + 1) * d, :], sem.at[c]))
        for cp in copies:
            cp.start()
        for cp in copies:
            cp.wait()


def mlp(lens, low, x, cot, gathered, wdown, vec):
    mb, rows, d = x.shape
    ff = wdown.shape[0]
    nb = rows // ROWS

    def blk(m, i, ln):
        return (m, jnp.minimum(i, last_block(ln, m)), 0)

    def full(m, i, ln):
        return (m, i, 0)

    one = pl.Buffered(1)
    return pl.pallas_call(
        mlp_kernel,
        grid_spec=pltpu.PrefetchScalarGridSpec(
            num_scalar_prefetch=1,
            grid=(mb, nb),
            in_specs=[
                pl.BlockSpec((1, ROWS, d), blk),
                pl.BlockSpec((1, ROWS, d), blk),
                pl.BlockSpec((1, ROWS, d), blk),
                pl.BlockSpec((d, d), lambda m, i, ln: (0, 3), pipeline_mode=one),
                pl.BlockSpec((d, ff), lambda m, i, ln: (0, 1), pipeline_mode=one),
                pl.BlockSpec((ff, d), lambda m, i, ln: (0, 0), pipeline_mode=one),
                pl.BlockSpec((8, d), lambda m, i, ln: (0, 0)),
            ],
            out_specs=[
                pl.BlockSpec((1, ROWS, d), full),
                pl.BlockSpec((1, ROWS, d), blk),
                pl.BlockSpec((1, ROWS, d), blk),
                pl.BlockSpec((1, 16, ROWS), lambda m, i, ln: (m, 0, jnp.minimum(i, last_block(ln, m)))),
                pl.BlockSpec(memory_space=pl.ANY),
                pl.BlockSpec(memory_space=pl.ANY),
                pl.BlockSpec((8, d), lambda m, i, ln: (0, 0)),
            ],
            scratch_shapes=[
                pltpu.VMEM((d, d), F32),
                pltpu.VMEM((d, ff), F32),
                pltpu.VMEM((ff, d), F32),
                pltpu.VMEM((d, d + ff), BF),
                pltpu.SemaphoreType.DMA((ff // d,)),
            ],
        ),
        out_shape=[
            jax.ShapeDtypeStruct((mb, rows, d), BF),
            jax.ShapeDtypeStruct((mb, rows, d), F32),
            jax.ShapeDtypeStruct((mb, rows, d), BF),
            jax.ShapeDtypeStruct((mb, 16, rows), F32),
            jax.ShapeDtypeStruct((d, d + ff), BF),
            jax.ShapeDtypeStruct((ff, d), BF),
            jax.ShapeDtypeStruct((8, d), F32),
        ],
        compiler_params=params(2),
        name="mlp",
    )(lens, low, x, cot, gathered, gathered, wdown, vec)


def attn_bwd_kernel(lens, x_ref, q_ref, k_ref, v_ref, gmix_ref, gmid_ref, lse_ref, inner_ref,
                    w_ref, vec_ref, dx_ref, gw_ref, acc_ref, dk_ref, dv_ref, gq_ref, gvec_ref):
    m = pl.program_id(0)
    g = pl.program_id(1)
    i = pl.num_programs(1) - 1 - g
    d = x_ref.shape[2]
    end = last_block(lens, m)
    live = i <= end
    first = (m == 0) & (g == 0)
    final = (m == pl.num_programs(0) - 1) & (i == 0)

    @pl.when(first)
    def _():
        acc_ref[...] = jnp.zeros_like(acc_ref)
        gvec_ref[...] = jnp.zeros_like(gvec_ref)

    @pl.when(jnp.logical_not(live))
    def _():
        dx_ref[...] = jnp.zeros_like(dx_ref)

    lane = lax.broadcasted_iota(jnp.int32, (ROWS, 128), 1)
    key = lax.broadcasted_iota(jnp.int32, (ROWS, ROWS), 0)
    row = lax.broadcasted_iota(jnp.int32, (ROWS, ROWS), 1)

    def variant(ii):
        keys = (ii + 1) * ROWS

        @pl.when(live & (i == ii))
        def _():
            allowed = (key <= row) & (key + ii * ROWS < lens[m])
            fresh = end == ii

            def pair(hp, carry):
                at = pl.multiple_of(hp * 128, 128)
                q = q_ref[0, :, pl.ds(at, 128)].astype(F32) * 0.125
                gm = gmix_ref[0, :, pl.ds(at, 128)]
                k = k_ref[0, 0:keys, pl.ds(at, 128)]
                v = v_ref[0, 0:keys, pl.ds(at, 128)]
                k_t = jnp.transpose(k)
                probs, grads, qs, gms, dqs = [], [], [], [], []
                for h in range(2):
                    mine = (lane < 64) == (h == 0)
                    qh = jnp.where(mine, q, 0.0).astype(BF)
                    gh = jnp.where(mine, gm, jnp.zeros_like(gm))
                    s = dot(k, qh, 1, 1)
                    tail = jnp.where(allowed, s[ii * ROWS:], -1e30)
                    s = tail if ii == 0 else jnp.concatenate([s[:ii * ROWS], tail], axis=0)
                    p = jnp.exp(s - lse_ref[0, pl.ds(hp * 2 + h, 1), :])
                    dp = dot(v, gh, 1, 1)
                    ds = (p * (dp - inner_ref[0, pl.ds(hp * 2 + h, 1), :])).astype(BF)
                    dqs.append(dot(k_t, ds)[h * 64:(h + 1) * 64])
                    probs.append(p.astype(BF))
                    grads.append(ds)
                    qs.append(qh)
                    gms.append(gh)
                dv = dot(jnp.concatenate(probs, axis=1), jnp.concatenate(gms, axis=0))
                dk = dot(jnp.concatenate(grads, axis=1), jnp.concatenate(qs, axis=0))
                dq = jnp.transpose(jnp.concatenate(dqs, axis=0)) * 0.125
                gq_ref[:, pl.ds(at, 128)] = dq.astype(BF)
                span = pl.ds(at, 128)
                dv_ref[0:keys, span] = jnp.where(fresh, 0.0, dv_ref[0:keys, span]) + dv
                dk_ref[0:keys, span] = jnp.where(fresh, 0.0, dk_ref[0:keys, span]) + dk
                return carry

            lax.fori_loop(0, d // 128, pair, 0)

    for ii in range(x_rows_blocks(dk_ref)):
        variant(ii)

    @pl.when(live)
    def _():
        base = pl.ds(pl.multiple_of(i * ROWS, ROWS), ROWS)
        gq_ref[:, d:2 * d] = dk_ref[base, :].astype(BF)
        gq_ref[:, 2 * d:] = dv_ref[base, :].astype(BF)
        n1, r1 = norm(x_ref[0].astype(F32))
        gain = vec_ref[0:1, :]
        low_t = jnp.transpose((n1 * gain + vec_ref[1:2, :]).astype(BF))
        e1 = jnp.zeros((ROWS, d), F32)
        for t in range(3):
            at = slice(t * d, (t + 1) * d)
            gq = gq_ref[:, at]
            e1 = e1 + dot(gq, w_ref[:, at], 1, 1)
            acc_ref[:, at] += dot(low_t, gq)
        gvec_ref[0:1, :] += jnp.sum(e1 * n1, axis=0, keepdims=True)
        gvec_ref[1:2, :] += jnp.sum(e1, axis=0, keepdims=True)
        alive = lax.broadcasted_iota(jnp.int32, (ROWS, 1), 0) + i * ROWS < lens[m]
        dx = gmid_ref[0] + norm_back(e1 * gain, n1, r1)
        dx_ref[0] = jnp.where(alive, dx, 0.0).astype(BF)

    @pl.when(final)
    def _():
        gw_ref[:, 0:3 * d] = acc_ref[...].astype(BF)
        gw_ref[:, 3 * d:] = jnp.transpose(gvec_ref[...]).astype(BF)


def attn_bwd(lens, x, qkv, gmix, gmid, lse, inner, gathered, vec):
    mb, rows, d = x.shape
    nb = rows // ROWS

    def blk(m, g, ln):
        return (m, jnp.minimum(nb - 1 - g, last_block(ln, m)), 0)

    def stat(m, g, ln):
        return (m, 0, jnp.minimum(nb - 1 - g, last_block(ln, m)))

    one = pl.Buffered(1)
    return pl.pallas_call(
        attn_bwd_kernel,
        grid_spec=pltpu.PrefetchScalarGridSpec(
            num_scalar_prefetch=1,
            grid=(mb, nb),
            in_specs=[
                pl.BlockSpec((1, ROWS, d), blk),
                pl.BlockSpec((1, ROWS, d), blk),
                pl.BlockSpec((1, rows, d), lambda m, g, ln: (m, 0, 1)),
                pl.BlockSpec((1, rows, d), lambda m, g, ln: (m, 0, 2)),
                pl.BlockSpec((1, ROWS, d), blk),
                pl.BlockSpec((1, ROWS, d), blk),
                pl.BlockSpec((1, 16, ROWS), stat),
                pl.BlockSpec((1, 16, ROWS), stat),
                pl.BlockSpec((d, 3 * d), lambda m, g, ln: (0, 0), pipeline_mode=one),
                pl.BlockSpec((8, d), lambda m, g, ln: (0, 0)),
            ],
            out_specs=[
                pl.BlockSpec((1, ROWS, d), lambda m, g, ln: (m, nb - 1 - g, 0)),
                pl.BlockSpec((d, 3 * d + 128), lambda m, g, ln: (0, 0), pipeline_mode=one),
            ],
            scratch_shapes=[
                pltpu.VMEM((d, 3 * d), F32),
                pltpu.VMEM((rows, d), F32),
                pltpu.VMEM((rows, d), F32),
                pltpu.VMEM((ROWS, 3 * d), BF),
                pltpu.VMEM((128, d), F32),
            ],
        ),
        out_shape=[
            jax.ShapeDtypeStruct((mb, rows, d), BF),
            jax.ShapeDtypeStruct((d, 3 * d + 128), BF),
        ],
        compiler_params=params(2),
        name="attn_bwd",
    )(lens, x, qkv, qkv, qkv, gmix, gmid, lse, inner, gathered, vec)


def swap(x, axis, bits):
    size = lax.axis_size(axis)
    return lax.ppermute(x, axis, [(s, s ^ bits) for s in range(size)])


def exchange(parts, axis):
    size = lax.axis_size(axis)
    return [parts[0]] + [swap(parts[b], axis, b) for b in range(1, size)]


def staged_sum(grads):
    dp = lax.axis_size("dp")
    zs = lax.axis_size("fsdp")
    width = grads.shape[1]
    block = grads.reshape(dp // 2, 2, zs, -1, width)
    place = lax.axis_index("dp")
    core = place % 2
    chip = place // 2
    mine = lax.dynamic_index_in_dim(block, core, 1, keepdims=False)
    other = lax.dynamic_index_in_dim(block, 1 - core, 1, keepdims=False)
    total = (mine.astype(F32) + swap(other, "dp", 1).astype(F32)).astype(BF)
    acc = lax.dynamic_index_in_dim(total, chip, 0, keepdims=False).astype(F32)
    for b in range(1, dp // 2):
        part = lax.dynamic_index_in_dim(total, chip ^ b, 0, keepdims=False)
        acc = acc + swap(part, "dp", 2 * b).astype(F32)
    low = acc.astype(BF)
    z = lax.axis_index("fsdp")
    acc = lax.dynamic_index_in_dim(low, z, 0, keepdims=False).astype(F32)
    for b in range(1, zs):
        part = lax.dynamic_index_in_dim(low, z ^ b, 0, keepdims=False)
        acc = acc + swap(part, "fsdp", b).astype(F32)
    return acc


def per_device(tokens, cotangent, lengths, perm, ln1_gain, ln1_bias, w_qkv, w_out,
               ln2_gain, ln2_bias, w_up, w_down):
    zs = lax.axis_size("fsdp")
    devices = lax.axis_size("dp") * zs
    z = lax.axis_index("fsdp")
    slots, rows, d = tokens.shape
    mb = slots // zs
    ff = w_up.shape[1]
    share = w_qkv.shape[0]
    chunks = ff // d
    dealing = perm[0]
    lens = lax.dynamic_slice_in_dim(lengths[0], z * mb, mb)
    order = (z ^ lax.iota(jnp.int32, zs))
    take_at = (order[:, None] * mb + lax.iota(jnp.int32, mb)[None, :]).reshape(-1)
    send_at = jnp.take(dealing, take_at, mode="clip")

    vectors = jnp.stack([ln1_gain, ln1_bias, ln2_gain, ln2_bias], axis=1)
    vectors = jnp.pad(vectors, ((0, 0), (0, 124)))
    down = w_down.reshape(chunks, share, d).transpose(1, 0, 2).reshape(share, ff)
    shard = jnp.concatenate([w_qkv, w_out, w_up, down, vectors], axis=1)
    gathered = lax.all_gather(shard, ("dp", "fsdp"), axis=0, tiled=True)
    first = w_qkv.shape[1] + w_out.shape[1] + ff
    wdown = gathered[:, first:first + ff].reshape(devices, share, chunks, d)
    wdown = wdown.transpose(0, 2, 1, 3).reshape(ff, d)
    vec = jnp.pad(jnp.transpose(gathered[:, first + ff:first + ff + 4]).astype(F32), ((0, 4), (0, 0)))

    def deal(array):
        picked = jnp.take(array, send_at, axis=0, mode="clip").reshape(zs, mb, rows, d)
        got = jnp.stack(exchange([picked[b] for b in range(zs)], "fsdp"))
        got = jnp.take(got, order, axis=0, mode="clip")
        return got.transpose(1, 0, 2, 3).reshape(mb, zs * rows, d)

    inverse = jnp.zeros((slots,), jnp.int32).at[dealing].set(lax.iota(jnp.int32, slots))
    back_at = ((inverse // mb) ^ z) * mb + inverse % mb

    def give_back(array):
        split = array.reshape(mb, zs, rows, d)
        parts = [lax.dynamic_index_in_dim(split, z ^ b, 1, keepdims=False) for b in range(zs)]
        got = jnp.concatenate(exchange(parts, "fsdp"), axis=0)
        return jnp.take(got, back_at, axis=0, mode="clip")

    x = deal(tokens)
    cot = deal(cotangent)
    qkv, low, lse = attn_fwd(lens, x, gathered, vec)
    out, gmid, gmix, inner, gmain, gdown, gvec2 = mlp(lens, low, x, cot, gathered, wdown, vec)
    gdown = gdown.reshape(devices, chunks, share, d).transpose(0, 2, 1, 3).reshape(d, ff)
    gcol = jnp.pad(jnp.transpose(gvec2[0:2]), ((0, 0), (0, 126))).astype(BF)
    early = jnp.concatenate([gmain, gdown, gcol], axis=1)
    early = lax.psum_scatter(early, ("dp", "fsdp"), scatter_dimension=0, tiled=True)
    block_out = give_back(out)
    dx, gw = attn_bwd(lens, x, qkv, gmix, gmid, lse, inner, gathered, vec)
    d_tokens = give_back(dx)
    late = staged_sum(gw)
    early = early.astype(F32)
    g_down = early[:, d + ff:d + 2 * ff].reshape(share, chunks, d).transpose(1, 0, 2).reshape(share * chunks, d)
    return (
        block_out,
        d_tokens,
        late[:, 3 * d],
        late[:, 3 * d + 1],
        late[:, :3 * d],
        early[:, :d],
        early[:, d + 2 * ff],
        early[:, d + 2 * ff + 1],
        early[:, d:d + ff],
        g_down,
    )


def solution(mesh):
    wide = P(("dp", "fsdp"), None)
    thin = P(("dp", "fsdp"))
    seq = P("dp", "fsdp", None)
    group = P("dp", None)
    return jax.shard_map(
        per_device,
        mesh=mesh,
        in_specs=(seq, seq, group, group, thin, thin, wide, wide, thin, thin, wide, wide),
        out_specs=(seq, seq, thin, thin, wide, wide, thin, thin, wide, wide),
        check_vma=False,
    )
```

```python
import functools
import math

import jax
import jax.numpy as jnp
from jax import lax
from jax.experimental import pallas as pl
from jax.experimental.pallas import tpu as pltpu
from jax.sharding import PartitionSpec as P


DEPTH = 48
EPS = 1e-05
ROWS = 256
HALF = 128
GROUP = 3
BF = jnp.bfloat16
F32 = jnp.float32
ALPHA = 1.0 / math.sqrt(DEPTH)
GELU_C = 0.7978845608028654
GELU_A = 0.044715
VMEM_LIMIT = 60 * 1024 * 1024


def dot(a, b, ca=1, cb=0):
    return lax.dot_general(a, b, (((ca,), (cb,)), ((), ())), preferred_element_type=F32)


def norm(v):
    c = v - jnp.mean(v, axis=-1, keepdims=True)
    r = lax.rsqrt(jnp.mean(c * c, axis=-1, keepdims=True) + EPS)
    return c * r, r


def norm_back(f, n, r):
    return r * (f - jnp.mean(f, axis=-1, keepdims=True) - n * jnp.mean(f * n, axis=-1, keepdims=True))


def params(n):
    return pltpu.CompilerParams(
        dimension_semantics=("arbitrary",) * n, vmem_limit_bytes=VMEM_LIMIT
    )


def cost(micros, moved):
    return pl.CostEstimate(flops=int(micros * 1e9), transcendentals=0, bytes_accessed=moved)


def last_block(lens, m):
    return (lens[m] + (ROWS - 1)) // ROWS - 1


def attn_fwd_kernel(lens, x_ref, w_ref, vec_ref, qkv_ref, low_ref, lse_ref, kv_ref):
    m = pl.program_id(0)
    i = pl.program_id(1)
    d = x_ref.shape[2]
    live = i <= last_block(lens, m)

    @pl.when(live)
    def _():
        n, _ = norm(x_ref[0].astype(F32))
        low = (n * vec_ref[0:1, :] + vec_ref[1:2, :]).astype(BF)
        for t in range(3):
            part = dot(low, w_ref[:, t * d:(t + 1) * d]).astype(BF)
            qkv_ref[0, :, t * d:(t + 1) * d] = part
            if t:
                kv_ref[pl.ds(pl.multiple_of(i * ROWS, ROWS), ROWS), (t - 1) * d:t * d] = part

    part = lens[m] - i * ROWS <= HALF

    def variant(ii, size):
        keys = ii * ROWS + size

        @pl.when(live & (i == ii) & (part == (size == HALF)))
        def _():
            lane = lax.broadcasted_iota(jnp.int32, (size, 128), 1)
            row = lax.broadcasted_iota(jnp.int32, (size, size), 0)
            key = lax.broadcasted_iota(jnp.int32, (size, size), 1)
            allowed = (key <= row) & (key + ii * ROWS < lens[m])

            def group(gp, cols):
                spans, scores, values = [], [], []
                for sub in range(GROUP):
                    at = pl.multiple_of((gp * GROUP + sub) * 128, 128)
                    spans.append(pl.ds(at, 128))
                    q = qkv_ref[0, 0:size, pl.ds(at, 128)].astype(F32) * 0.125
                    k = kv_ref[0:keys, pl.ds(at, 128)]
                    values.append(kv_ref[0:keys, pl.ds(pl.multiple_of(d + at, 128), 128)])
                    for h in range(2):
                        qh = jnp.where((lane < 64) == (h == 0), q, 0.0).astype(BF)
                        scores.append(dot(qh, k, 1, 1))
                outs = []
                for n, s in enumerate(scores):
                    tail = jnp.where(allowed, s[:, ii * ROWS:], -1e30)
                    s = tail if ii == 0 else jnp.concatenate([s[:, :ii * ROWS], tail], axis=1)
                    peak = jnp.max(s, axis=-1, keepdims=True)
                    e = jnp.exp(s - peak)
                    total = jnp.sum(e, axis=-1, keepdims=True)
                    p = (e * (1.0 / total)).astype(BF)
                    outs.append(dot(p, values[n // 2]))
                    cols = jnp.where(lane == gp * (2 * GROUP) + n, peak + jnp.log(total), cols)
                for sub, span in enumerate(spans):
                    low_ref[0, 0:size, span] = jnp.where(lane < 64, outs[2 * sub], outs[2 * sub + 1]).astype(BF)
                return cols

            cols = lax.fori_loop(0, d // (128 * GROUP), group, jnp.zeros((size, 128), F32))
            lse_ref[0, :, 0:size] = jnp.transpose(cols)[0:16]

    for ii in range(x_rows_blocks(kv_ref)):
        variant(ii, ROWS)
        if ii:
            variant(ii, HALF)


def x_rows_blocks(ref):
    return ref.shape[0] // ROWS


def attn_fwd(lens, x, w, vec):
    mb, rows, d = x.shape
    nb = rows // ROWS

    def blk(m, i, ln):
        return (m, jnp.minimum(i, last_block(ln, m)), 0)

    return pl.pallas_call(
        attn_fwd_kernel,
        grid_spec=pltpu.PrefetchScalarGridSpec(
            num_scalar_prefetch=1,
            grid=(mb, nb),
            in_specs=[
                pl.BlockSpec((1, ROWS, d), blk),
                pl.BlockSpec((d, 3 * d), lambda m, i, ln: (0, 0), pipeline_mode=pl.Buffered(1)),
                pl.BlockSpec((8, d), lambda m, i, ln: (0, 0)),
            ],
            out_specs=[
                pl.BlockSpec((1, ROWS, 3 * d), blk),
                pl.BlockSpec((1, ROWS, d), blk),
                pl.BlockSpec((1, 16, ROWS), lambda m, i, ln: (m, 0, jnp.minimum(i, last_block(ln, m)))),
            ],
            scratch_shapes=[pltpu.VMEM((rows, 2 * d), BF)],
        ),
        out_shape=[
            jax.ShapeDtypeStruct((mb, rows, 3 * d), BF),
            jax.ShapeDtypeStruct((mb, rows, d), BF),
            jax.ShapeDtypeStruct((mb, 16, rows), F32),
        ],
        compiler_params=params(2),
        cost_estimate=cost(60, 20 << 20),
        name="attn_fwd",
    )(lens, x, w, vec)


def weight_copies(rest_ref, down_ref, wout_ref, wup_ref, wdown_ref, sem):
    d = wout_ref.shape[0]
    ff = wup_ref.shape[1]
    chunks = ff // d

    def out():
        return pltpu.make_async_copy(rest_ref.at[:, ff:ff + d], wout_ref, sem.at[2 * chunks])

    def up(c):
        at = pl.ds(pl.multiple_of(c * d, 128), d)
        return pltpu.make_async_copy(rest_ref.at[:, at], wup_ref.at[:, at], sem.at[c])

    def down(c):
        at = pl.ds(pl.multiple_of(c * d, 128), d)
        return pltpu.make_async_copy(down_ref.at[at, :], wdown_ref.at[at, :], sem.at[chunks + c])

    def start():
        out().start()
        for c in range(chunks):
            up(c).start()
            down(c).start()

    return start, out, up, down


def run_chunks(chunk, count, opening):
    if opening:
        lax.fori_loop(0, count, chunk, 0)
    else:
        for c in range(count):
            chunk(c, 0)


def mlp_fwd_kernel(lens, low_ref, x_ref, vec_ref, rest_ref, down_ref, out_ref, mid_ref,
                   wout_ref, wup_ref, wdown_ref, y_ref, sem):
    m = pl.program_id(0)
    i = pl.program_id(1)
    d = x_ref.shape[2]
    live = i <= last_block(lens, m)
    part = lens[m] - i * ROWS <= HALF
    first = (m == 0) & (i == 0)
    start, get_out, get_up, get_down = weight_copies(rest_ref, down_ref, wout_ref, wup_ref, wdown_ref, sem)

    @pl.when(first)
    def _():
        start()
        get_out().wait()

    @pl.when(jnp.logical_not(live))
    def _():
        out_ref[...] = jnp.zeros_like(out_ref)

    def body(size, opening):
        @pl.when(live & (part == (size == HALF)) & (first == opening))
        def _():
            alive = lax.broadcasted_iota(jnp.int32, (size, 1), 0) + i * ROWS < lens[m]
            middle = x_ref[0, 0:size].astype(F32) + ALPHA * dot(low_ref[0, 0:size], wout_ref[...])
            mid_ref[0, 0:size] = middle
            n2, _ = norm(middle)
            second = (n2 * vec_ref[2:3, :] + vec_ref[3:4, :]).astype(BF)
            y_ref[0:size] = jnp.zeros((size, d), F32)

            def chunk(c, carry):
                if opening:
                    get_up(c).wait()
                    get_down(c).wait()
                    at = pl.ds(pl.multiple_of(c * d, 128), d)
                else:
                    at = slice(c * d, (c + 1) * d)
                up = dot(second, wup_ref[:, at])
                t = jnp.tanh(GELU_C * (up + GELU_A * up * up * up))
                y_ref[0:size] += dot((up * (0.5 * (1.0 + t))).astype(BF), wdown_ref[at, :])
                return carry

            run_chunks(chunk, wup_ref.shape[1] // d, opening)
            out_ref[0, 0:size] = jnp.where(alive, middle + ALPHA * y_ref[0:size], 0.0).astype(BF)
            if size < ROWS:
                out_ref[0, size:] = jnp.zeros((ROWS - size, d), BF)

    body(ROWS, True)
    body(ROWS, False)
    body(HALF, False)


def mlp_fwd(lens, low, x, rest, wdown, vec):
    mb, rows, d = x.shape
    ff = wdown.shape[0]

    def blk(m, i, ln):
        return (m, jnp.minimum(i, last_block(ln, m)), 0)

    return pl.pallas_call(
        mlp_fwd_kernel,
        grid_spec=pltpu.PrefetchScalarGridSpec(
            num_scalar_prefetch=1,
            grid=(mb, rows // ROWS),
            in_specs=[
                pl.BlockSpec((1, ROWS, d), blk),
                pl.BlockSpec((1, ROWS, d), blk),
                pl.BlockSpec((8, d), lambda m, i, ln: (0, 0)),
                pl.BlockSpec(memory_space=pl.ANY),
                pl.BlockSpec(memory_space=pl.ANY),
            ],
            out_specs=[
                pl.BlockSpec((1, ROWS, d), lambda m, i, ln: (m, i, 0)),
                pl.BlockSpec((1, ROWS, d), blk),
            ],
            scratch_shapes=[
                pltpu.VMEM((d, d), BF),
                pltpu.VMEM((d, ff), BF),
                pltpu.VMEM((ff, d), BF),
                pltpu.VMEM((ROWS, d), F32),
                pltpu.SemaphoreType.DMA((2 * (ff // d) + 1,)),
            ],
        ),
        out_shape=[
            jax.ShapeDtypeStruct((mb, rows, d), BF),
            jax.ShapeDtypeStruct((mb, rows, d), F32),
        ],
        compiler_params=params(2),
        cost_estimate=cost(40, 40 << 20),
        name="mlp_fwd",
    )(lens, low, x, vec, rest, wdown)


def mlp_bwd_kernel(lens, low_ref, mid_ref, cot_ref, vec_ref, rest_ref, wd_ref,
                   gmid_ref, gmix_ref, inner_ref, gmain_ref, gdown_ref,
                   wout_ref, wup_ref, wdown_ref, aout_ref, aup_ref, adown_ref, gvec_ref, e2_ref,
                   stage_ref, down_ref, sem, *, share):
    m = pl.program_id(0)
    i = pl.program_id(1)
    d = mid_ref.shape[2]
    ff = wup_ref.shape[1]
    chunks = ff // d
    live = i <= last_block(lens, m)
    part = lens[m] - i * ROWS <= HALF
    first = (m == 0) & (i == 0)
    final = (m == pl.num_programs(0) - 1) & (i == pl.num_programs(1) - 1)
    start, get_out, get_up, get_down = weight_copies(rest_ref, wd_ref, wout_ref, wup_ref, wdown_ref, sem)

    @pl.when(first)
    def _():
        start()
        aout_ref[...] = jnp.zeros_like(aout_ref)
        aup_ref[...] = jnp.zeros_like(aup_ref)
        adown_ref[...] = jnp.zeros_like(adown_ref)
        gvec_ref[...] = jnp.zeros_like(gvec_ref)
        get_out().wait()

    def body(size):
        @pl.when(live & (part == (size == HALF)))
        def _():
            alive = lax.broadcasted_iota(jnp.int32, (size, 1), 0) + i * ROWS < lens[m]
            low = low_ref[0, 0:size]
            n2, r2 = norm(mid_ref[0, 0:size])
            gain = vec_ref[2:3, :]
            second = (n2 * gain + vec_ref[3:4, :]).astype(BF)
            second_t = jnp.transpose(second)
            gout = jnp.where(alive, cot_ref[0, 0:size].astype(F32), 0.0)
            gmlp = (ALPHA * gout).astype(BF)
            e2_ref[0:size] = jnp.zeros((size, d), F32)

            def chunk(c, carry):
                @pl.when(first)
                def _():
                    get_up(c).wait()
                    get_down(c).wait()

                at = pl.ds(pl.multiple_of(c * d, 128), d)
                up = dot(second, wup_ref[:, at])
                back = dot(gmlp, wdown_ref[at, :], 1, 1)
                sq = up * up
                t = jnp.tanh(GELU_C * (up + GELU_A * sq * up))
                half = 0.5 * (1.0 + t)
                act = (up * half).astype(BF)
                slope = half + 0.5 * up * (1.0 - t * t) * (GELU_C * (1.0 + 3.0 * GELU_A * sq))
                gup = (back * slope).astype(BF)
                adown_ref[at, :] += dot(act, gmlp, 0, 0)
                e2_ref[0:size] += dot(gup, wup_ref[:, at], 1, 1)
                aup_ref[:, at] += dot(second_t, gup)
                return carry

            lax.fori_loop(0, chunks, chunk, 0)
            e2 = e2_ref[0:size]
            gvec_ref[0:1, :] += jnp.sum(e2 * n2, axis=0, keepdims=True)
            gvec_ref[1:2, :] += jnp.sum(e2, axis=0, keepdims=True)
            gmid = gout + norm_back(e2 * gain, n2, r2)
            gmid_ref[0, 0:size] = gmid
            gao = (ALPHA * gmid).astype(BF)
            gmix = dot(gao, wout_ref[...], 1, 1).astype(BF)
            aout_ref[...] += dot(low, gao, 0, 0)
            gmix_ref[0, 0:size] = gmix
            prod = gmix.astype(F32) * low.astype(F32)
            head = lax.broadcasted_iota(jnp.int32, (16, d), 0)
            lane = lax.broadcasted_iota(jnp.int32, (16, d), 1)
            pick = jnp.where(lane // 64 == head, 1.0, 0.0).astype(F32)
            inner_ref[0, :, 0:size] = lax.dot_general(
                pick, prod, (((1,), (1,)), ((), ())),
                preferred_element_type=F32, precision=lax.Precision.HIGHEST,
            )

    body(ROWS)
    body(HALF)

    @pl.when(final)
    def _():
        main = d + ff
        stage_ref[:, 0:d] = aout_ref[...].astype(BF)
        stage_ref[:, d:main] = aup_ref[...].astype(BF)
        send = pltpu.make_async_copy(stage_ref, gmain_ref, sem.at[0])
        send.start()
        if share % 8 == 0:

            def regroup(e, carry):
                for c in range(chunks):
                    at = 2 * chunks * share * e + c * share
                    one = adown_ref[pl.ds(pl.multiple_of(at, 8), share), :]
                    two = adown_ref[pl.ds(pl.multiple_of(at + chunks * share, 8), share), :]
                    both = jnp.concatenate([one, two], axis=0).astype(BF)
                    down_ref[pl.ds(pl.multiple_of(2 * share * e, 16), 2 * share), c * d:(c + 1) * d] = both
                return carry

            lax.fori_loop(0, d // (2 * share), regroup, 0)
        else:
            for c in range(chunks):
                down_ref[:, c * d:(c + 1) * d] = adown_ref[c * d:(c + 1) * d, :].astype(BF)
        down_ref[:, ff:ff + 128] = jnp.transpose(gvec_ref[...]).astype(BF)
        last = pltpu.make_async_copy(down_ref, gdown_ref, sem.at[1])
        last.start()
        send.wait()
        last.wait()


def mlp_bwd(lens, low, mid, cot, rest, wdown, vec, share):
    mb, rows, d = mid.shape
    ff = wdown.shape[0]

    def blk(m, i, ln):
        return (m, jnp.minimum(i, last_block(ln, m)), 0)

    return pl.pallas_call(
        functools.partial(mlp_bwd_kernel, share=share),
        grid_spec=pltpu.PrefetchScalarGridSpec(
            num_scalar_prefetch=1,
            grid=(mb, rows // ROWS),
            in_specs=[
                pl.BlockSpec((1, ROWS, d), blk),
                pl.BlockSpec((1, ROWS, d), blk),
                pl.BlockSpec((1, ROWS, d), blk),
                pl.BlockSpec((8, d), lambda m, i, ln: (0, 0)),
                pl.BlockSpec(memory_space=pl.ANY),
                pl.BlockSpec(memory_space=pl.ANY),
            ],
            out_specs=[
                pl.BlockSpec((1, ROWS, d), blk),
                pl.BlockSpec((1, ROWS, d), blk),
                pl.BlockSpec((1, 16, ROWS), lambda m, i, ln: (m, 0, jnp.minimum(i, last_block(ln, m)))),
                pl.BlockSpec(memory_space=pl.ANY),
                pl.BlockSpec(memory_space=pl.ANY),
            ],
            scratch_shapes=[
                pltpu.VMEM((d, d), BF),
                pltpu.VMEM((d, ff), BF),
                pltpu.VMEM((ff, d), BF),
                pltpu.VMEM((d, d), F32),
                pltpu.VMEM((d, ff), F32),
                pltpu.VMEM((ff, d), F32),
                pltpu.VMEM((128, d), F32),
                pltpu.VMEM((ROWS, d), F32),
                pltpu.VMEM((d, d + ff), BF),
                pltpu.VMEM((d, ff + 128), BF),
                pltpu.SemaphoreType.DMA((2 * (ff // d) + 1,)),
            ],
        ),
        out_shape=[
            jax.ShapeDtypeStruct((mb, rows, d), F32),
            jax.ShapeDtypeStruct((mb, rows, d), BF),
            jax.ShapeDtypeStruct((mb, 16, rows), F32),
            jax.ShapeDtypeStruct((d, d + ff), BF),
            jax.ShapeDtypeStruct((d, ff + 128), BF),
        ],
        compiler_params=params(2),
        cost_estimate=cost(80, 60 << 20),
        name="mlp_bwd",
    )(lens, low, mid, cot, vec, rest, wdown)


def attn_bwd_kernel(lens, x_ref, q_ref, k_ref, v_ref, gmix_ref, gmid_ref, lse_ref, inner_ref,
                    w_ref, vec_ref, *rest, m, begin):
    if begin:
        dx_ref, gw_ref, acc_ref, gvec_ref, dk_ref, dv_ref, gq_ref = rest
    else:
        prev_ref, dx_ref, gw_ref, acc_ref, gvec_ref, dk_ref, dv_ref, gq_ref, before_ref, sem = rest
    g = pl.program_id(0)
    i = pl.num_programs(0) - 1 - g
    d = x_ref.shape[2]
    end = last_block(lens, m)
    live = i <= end

    @pl.when(g == 0)
    def _():
        if not begin:
            pltpu.make_async_copy(prev_ref, before_ref, sem).start()
        acc_ref[...] = jnp.zeros_like(acc_ref)
        gvec_ref[...] = jnp.zeros_like(gvec_ref)

    @pl.when(jnp.logical_not(live))
    def _():
        dx_ref[...] = jnp.zeros_like(dx_ref)

    part = lens[m] - i * ROWS <= HALF

    def variant(ii, size):
        keys = ii * ROWS + size

        @pl.when(live & (i == ii) & (part == (size == HALF)))
        def _():
            lane = lax.broadcasted_iota(jnp.int32, (size, 128), 1)
            key = lax.broadcasted_iota(jnp.int32, (size, size), 0)
            row = lax.broadcasted_iota(jnp.int32, (size, size), 1)
            allowed = (key <= row) & (key + ii * ROWS < lens[m])
            fresh = end == ii

            def group(gp, carry):
                spans, keep = [], []
                for sub in range(GROUP):
                    hp = gp * GROUP + sub
                    span = pl.ds(pl.multiple_of(hp * 128, 128), 128)
                    spans.append(span)
                    q = q_ref[0, 0:size, span].astype(F32) * 0.125
                    gm = gmix_ref[0, 0:size, span]
                    k = k_ref[0, 0:keys, span]
                    v = v_ref[0, 0:keys, span]
                    for h in range(2):
                        mine = (lane < 64) == (h == 0)
                        qh = jnp.where(mine, q, 0.0).astype(BF)
                        gh = jnp.where(mine, gm, jnp.zeros_like(gm))
                        keep.append((hp * 2 + h, qh, gh, dot(k, qh, 1, 1), dot(v, gh, 1, 1)))
                results = []
                for sub in range(GROUP):
                    k_t = jnp.transpose(k_ref[0, 0:keys, spans[sub]])
                    probs, grads, dqs = [], [], []
                    for h in range(2):
                        head, _, _, s, dp = keep[2 * sub + h]
                        tail = jnp.where(allowed, s[ii * ROWS:], -1e30)
                        s = tail if ii == 0 else jnp.concatenate([s[:ii * ROWS], tail], axis=0)
                        p = jnp.exp(s - lse_ref[0, pl.ds(head, 1), :][:, 0:size])
                        ds = (p * (dp - inner_ref[0, pl.ds(head, 1), :][:, 0:size])).astype(BF)
                        dqs.append(dot(k_t, ds)[h * 64:(h + 1) * 64])
                        probs.append(p.astype(BF))
                        grads.append(ds)
                    both = keep[2 * sub:2 * sub + 2]
                    dv = dot(jnp.concatenate(probs, axis=1), jnp.concatenate([b[2] for b in both], axis=0))
                    dk = dot(jnp.concatenate(grads, axis=1), jnp.concatenate([b[1] for b in both], axis=0))
                    dq = jnp.transpose(jnp.concatenate(dqs, axis=0)) * 0.125
                    results.append((dq, dk, dv))
                for span, (dq, dk, dv) in zip(spans, results):
                    gq_ref[0:size, span] = dq.astype(BF)
                    dv_ref[0:keys, span] = jnp.where(fresh, 0.0, dv_ref[0:keys, span]) + dv
                    dk_ref[0:keys, span] = jnp.where(fresh, 0.0, dk_ref[0:keys, span]) + dk
                return carry

            lax.fori_loop(0, d // (128 * GROUP), group, 0)

    for ii in range(x_rows_blocks(dk_ref)):
        variant(ii, ROWS)
        if ii:
            variant(ii, HALF)

    def finish(size):
        @pl.when(live & (part == (size == HALF)))
        def _():
            base = pl.ds(pl.multiple_of(i * ROWS, ROWS), size)
            gq_ref[0:size, d:2 * d] = dk_ref[base, :].astype(BF)
            gq_ref[0:size, 2 * d:] = dv_ref[base, :].astype(BF)
            n1, r1 = norm(x_ref[0, 0:size].astype(F32))
            gain = vec_ref[0:1, :]
            low_t = jnp.transpose((n1 * gain + vec_ref[1:2, :]).astype(BF))
            e1 = jnp.zeros((size, d), F32)
            for t in range(3):
                at = slice(t * d, (t + 1) * d)
                gq = gq_ref[0:size, at]
                e1 = e1 + dot(gq, w_ref[:, at], 1, 1)
                acc_ref[:, at] += dot(low_t, gq)
            gvec_ref[0:1, :] += jnp.sum(e1 * n1, axis=0, keepdims=True)
            gvec_ref[1:2, :] += jnp.sum(e1, axis=0, keepdims=True)
            alive = lax.broadcasted_iota(jnp.int32, (size, 1), 0) + i * ROWS < lens[m]
            dx = gmid_ref[0, 0:size] + norm_back(e1 * gain, n1, r1)
            dx_ref[0, 0:size] = jnp.where(alive, dx, 0.0).astype(BF)
            if size < ROWS:
                dx_ref[0, size:] = jnp.zeros((ROWS - size, d), BF)

    finish(ROWS)
    finish(HALF)

    @pl.when(i == 0)
    def _():
        total = acc_ref[...]
        rows = jnp.transpose(gvec_ref[...])
        if not begin:
            pltpu.make_async_copy(prev_ref, before_ref, sem).wait()
            total = total + before_ref[:, 0:3 * d].astype(F32)
            rows = rows + before_ref[:, 3 * d:].astype(F32)
        gw_ref[:, 0:3 * d] = total.astype(BF)
        gw_ref[:, 3 * d:] = rows.astype(BF)


def attn_bwd(m, prev, lens, x, qkv, gmix, gmid, lse, inner, gathered, vec):
    _, rows, d = x.shape
    nb = rows // ROWS
    begin = m == 0

    def blk(g, ln):
        return (m, jnp.minimum(nb - 1 - g, last_block(ln, m)), 0)

    def stat(g, ln):
        return (m, 0, jnp.minimum(nb - 1 - g, last_block(ln, m)))

    def fixed(g, ln):
        return (0, 0)

    one = pl.Buffered(1)
    whole = (d, 3 * d)
    wide = (d, 3 * d + 128)
    return pl.pallas_call(
        functools.partial(attn_bwd_kernel, m=m, begin=begin),
        grid_spec=pltpu.PrefetchScalarGridSpec(
            num_scalar_prefetch=1,
            grid=(nb,),
            in_specs=[
                pl.BlockSpec((1, ROWS, d), blk),
                pl.BlockSpec((1, ROWS, d), blk),
                pl.BlockSpec((1, rows, d), lambda g, ln: (m, 0, 1), pipeline_mode=one),
                pl.BlockSpec((1, rows, d), lambda g, ln: (m, 0, 2), pipeline_mode=one),
                pl.BlockSpec((1, ROWS, d), blk),
                pl.BlockSpec((1, ROWS, d), blk),
                pl.BlockSpec((1, 16, ROWS), stat),
                pl.BlockSpec((1, 16, ROWS), stat),
                pl.BlockSpec(whole, fixed, pipeline_mode=one),
                pl.BlockSpec((8, d), fixed),
            ] + ([] if begin else [pl.BlockSpec(memory_space=pl.ANY)]),
            out_specs=[
                pl.BlockSpec((1, ROWS, d), lambda g, ln: (0, nb - 1 - g, 0)),
                pl.BlockSpec(wide, fixed, pipeline_mode=one),
            ],
            scratch_shapes=[
                pltpu.VMEM(whole, F32),
                pltpu.VMEM((128, d), F32),
                pltpu.VMEM((rows, d), F32),
                pltpu.VMEM((rows, d), F32),
                pltpu.VMEM((ROWS, 3 * d), BF),
            ] + ([] if begin else [pltpu.VMEM(wide, BF), pltpu.SemaphoreType.DMA(())]),
        ),
        out_shape=[jax.ShapeDtypeStruct((1, rows, d), BF), jax.ShapeDtypeStruct(wide, BF)],
        compiler_params=params(1),
        cost_estimate=cost(40, 20 << 20),
        name="attn_bwd",
    )(lens, x, qkv, qkv, qkv, gmix, gmid, lse, inner, gathered, vec, *prev)


def place_blocks(table, pieces, blocks):
    each, rows, d = pieces[0].shape
    count = len(pieces)

    def kernel(at, *refs):
        srcs, out, held, sem = refs[:count], refs[count], refs[count + 1], refs[count + 2]
        slots = [(p, j, p * each + j) for p in range(count) for j in range(each)]
        loads = [pltpu.make_async_copy(srcs[p].at[j], held.at[k], sem.at[0, k]) for p, j, k in slots]
        stores = [pltpu.make_async_copy(held.at[k], out.at[at[k]], sem.at[1, k]) for p, j, k in slots]
        for c in loads:
            c.start()
        for load, store in zip(loads, stores):
            load.wait()
            store.start()
        for c in stores:
            c.wait()

    anywhere = pl.BlockSpec(memory_space=pl.ANY)
    return pl.pallas_call(
        kernel,
        grid_spec=pltpu.PrefetchScalarGridSpec(
            num_scalar_prefetch=1,
            grid=(1,),
            in_specs=[anywhere] * count,
            out_specs=anywhere,
            scratch_shapes=[
                pltpu.VMEM((count * each, rows, d), pieces[0].dtype),
                pltpu.SemaphoreType.DMA((2, count * each)),
            ],
        ),
        out_shape=jax.ShapeDtypeStruct((blocks, rows, d), pieces[0].dtype),
        compiler_params=params(1),
        cost_estimate=cost(4, 2 * blocks * rows * d * 2),
        name="place_blocks",
    )(table, *pieces)


def place_weights(table, sides, main, d):
    count, share, width = sides[0].shape
    chunks = (width - main) // d
    total = 2 * count * share

    def kernel(at, *refs):
        srcs, out, rest = refs[:2], refs[2], refs[3:]
        held, sem = rest[-2:]

        def load(side, k):
            return pltpu.make_async_copy(srcs[side].at[k], held.at[side, k], sem.at[side, k, chunks + 1])

        def stores(side, k):
            to = at[side * count + k]
            src = held.at[side, k]
            row = pl.ds(pl.multiple_of(to * share, 8), share)
            every = [pltpu.make_async_copy(src.at[:, 0:main], out.at[row, :], sem.at[side, k, 0])]
            for c in range(chunks):
                row = pl.ds(pl.multiple_of((to * chunks + c) * share, 8), share)
                col = slice(main + c * d, main + (c + 1) * d)
                every.append(pltpu.make_async_copy(src.at[:, col], rest[0].at[row, :], sem.at[side, k, c + 1]))
            return every

        for side in range(2):
            def begin(k, carry, side=side):
                load(side, k).start()
                return carry

            lax.fori_loop(0, count, begin, 0)
        for side in range(2):
            def turn(k, carry, side=side):
                load(side, k).wait()
                for c in stores(side, k):
                    c.start()
                return carry

            lax.fori_loop(0, count, turn, 0)
        for side in range(2):
            def end(k, carry, side=side):
                for c in stores(side, k):
                    c.wait()
                return carry

            lax.fori_loop(0, count, end, 0)

    anywhere = pl.BlockSpec(memory_space=pl.ANY)
    shapes = [jax.ShapeDtypeStruct((total, main), BF)]
    if chunks:
        shapes.append(jax.ShapeDtypeStruct((total * chunks, d), BF))
    return pl.pallas_call(
        kernel,
        grid_spec=pltpu.PrefetchScalarGridSpec(
            num_scalar_prefetch=1,
            grid=(1,),
            in_specs=[anywhere] * 2,
            out_specs=[anywhere] * len(shapes),
            scratch_shapes=[
                pltpu.VMEM((2, count, share, width), BF),
                pltpu.SemaphoreType.DMA((2, count, chunks + 2)),
            ],
        ),
        out_shape=shapes,
        compiler_params=params(1),
        cost_estimate=cost(8, 2 * total * width * 2),
        name="place_weights",
    )(table, *sides)


def swap(x, axis, bits):
    size = lax.axis_size(axis)
    return lax.ppermute(x, axis, [(s, s ^ bits) for s in range(size)])


def exchange(parts, axis):
    size = lax.axis_size(axis)
    return [parts[0]] + [swap(parts[b], axis, b) for b in range(1, size)]


def staged_gather(shard, main, d):
    dp = lax.axis_size("dp")
    zs = lax.axis_size("fsdp")
    chips = dp // 2
    got = jnp.stack(exchange([shard] * zs, "fsdp"))
    got = jnp.stack([got] + [swap(got, "dp", 2 * b) for b in range(1, chips)])
    share, width = shard.shape
    mine = got.reshape(chips * zs, share, width)
    other = swap(mine, "dp", 1)
    place = lax.axis_index("dp")
    z = lax.axis_index("fsdp")
    at = lax.iota(jnp.int32, chips * zs)
    table = jnp.concatenate([
        (place ^ (2 * (at // zs) + core)) * zs + (z ^ (at % zs)) for core in range(2)
    ])
    if share % 8 == 0:
        return place_weights(table, (mine, other), main, d)
    order = jnp.zeros_like(table).at[table].set(lax.iota(jnp.int32, dp * zs))
    whole = jnp.take(jnp.concatenate([mine, other]), order, axis=0, mode="clip")
    parts = [whole[:, :, :main].reshape(-1, main)]
    if width > main:
        down = whole[:, :, main:].reshape(dp * zs, share, -1, d).transpose(0, 2, 1, 3)
        parts.append(down.reshape(-1, d))
    return parts


def sum_partner(grads):
    dp = lax.axis_size("dp")
    block = grads.reshape(dp // 2, 2, -1, grads.shape[1])
    core = lax.axis_index("dp") % 2
    mine = lax.dynamic_index_in_dim(block, core, 1, keepdims=False)
    other = lax.dynamic_index_in_dim(block, 1 - core, 1, keepdims=False)
    return mine, swap(other, "dp", 1)


def sum_plane(mine, other):
    chip = lax.axis_index("dp") // 2

    def part(b):
        pick = [lax.dynamic_index_in_dim(t, chip ^ b, 0, keepdims=False) for t in (mine, other)]
        return (pick[0].astype(F32) + pick[1].astype(F32)).astype(BF)

    count = mine.shape[0]
    return [part(0)] + [swap(part(b), "dp", 2 * b) for b in range(1, count)]


def total_of(parts):
    acc = parts[0].astype(F32)
    for p in parts[1:]:
        acc = acc + p.astype(F32)
    return acc


def sum_line(parts):
    zs = lax.axis_size("fsdp")
    z = lax.axis_index("fsdp")
    low = total_of(parts).astype(BF)
    low = low.reshape(zs, -1, low.shape[1])
    pieces = [lax.dynamic_index_in_dim(low, z ^ b, 0, keepdims=False) for b in range(zs)]
    return total_of(exchange(pieces, "fsdp"))


def device_step(tokens, cotangent, lengths, perm, ln1_gain, ln1_bias, w_qkv, w_out,
               ln2_gain, ln2_bias, w_up, w_down):
    zs = lax.axis_size("fsdp")
    devices = lax.axis_size("dp") * zs
    z = lax.axis_index("fsdp")
    slots, rows, d = tokens.shape
    mb = slots // zs
    ff = w_up.shape[1]
    share = w_qkv.shape[0]
    chunks = ff // d
    dealing = perm[0]
    lens = lax.dynamic_slice_in_dim(lengths[0], z * mb, mb)
    order = (z ^ lax.iota(jnp.int32, zs))
    take_at = (order[:, None] * mb + lax.iota(jnp.int32, mb)[None, :]).reshape(-1)
    send_at = jnp.take(dealing, take_at, mode="clip")

    vectors = jnp.stack([ln1_gain, ln1_bias, ln2_gain, ln2_bias], axis=1)
    vectors = jnp.pad(vectors, ((0, 0), (0, 124)))
    down = w_down.reshape(chunks, share, d).transpose(1, 0, 2).reshape(share, ff)
    shard = jnp.concatenate([w_up, w_out, down], axis=1)
    (gathered,) = staged_gather(jnp.concatenate([w_qkv, vectors], axis=1), 3 * d + 128, d)
    rest, wdown = staged_gather(shard, ff + d, d)
    at = 3 * d
    vec = jnp.pad(jnp.transpose(gathered[:, at:at + 4]).astype(F32), ((0, 4), (0, 0)))

    def deal(array):
        parts = [jnp.take(array, send_at[b * mb:(b + 1) * mb], axis=0, mode="clip") for b in range(zs)]
        table = (lax.iota(jnp.int32, mb)[None, :] * zs + order[:, None]).reshape(-1)
        return place_blocks(table, exchange(parts, "fsdp"), slots).reshape(mb, zs * rows, d)

    def give_back(array):
        split = array.reshape(array.shape[0], zs, rows, d)
        parts = [lax.dynamic_index_in_dim(split, z ^ b, 1, keepdims=False) for b in range(zs)]
        return exchange(parts, "fsdp")

    x = deal(tokens)
    x, cotangent = lax.optimization_barrier((x, cotangent))
    cot = deal(cotangent)
    qkv, low, lse = attn_fwd(lens, x, gathered, vec)
    out, mid = mlp_fwd(lens, low, x, rest, wdown, vec)
    cot, out = lax.optimization_barrier((cot, out))
    gmid, gmix, inner, gmain, gdown = mlp_bwd(lens, low, mid, cot, rest, wdown, vec, share)
    if share % 8:
        gtop = gdown[:, :ff].reshape(d, chunks, d).transpose(1, 0, 2)
        gtop = gtop.reshape(devices, chunks, share, d).transpose(0, 2, 1, 3).reshape(d, ff)
        gdown = jnp.concatenate([gtop, gdown[:, ff:]], axis=1)
    early = lax.psum_scatter(gdown, ("dp", "fsdp"), scatter_dimension=0, tiled=True)
    halves = sum_partner(gmain)
    outs = give_back(out)
    grads = []
    prev = ()
    for m in range(mb):
        dx, gw = attn_bwd(m, prev, lens, x, qkv, gmix, gmid, lse, inner, gathered, vec)
        prev = (gw,)
        grads += give_back(dx)
        if m == 0:
            planes = sum_plane(*halves)
    halves = sum_partner(gw)
    late = sum_plane(*halves)
    late = sum_line(late)
    main = sum_line(planes)
    block_out = place_blocks(send_at, outs, slots)
    d_tokens = place_blocks(send_at.reshape(zs, mb).T.reshape(-1), grads, slots)
    early = early.astype(F32)
    g_down = early[:, :ff].reshape(share, chunks, d).transpose(1, 0, 2).reshape(share * chunks, d)
    return (
        block_out,
        d_tokens,
        late[:, 3 * d],
        late[:, 3 * d + 1],
        late[:, :3 * d],
        main[:, :d],
        early[:, ff],
        early[:, ff + 1],
        main[:, d:],
        g_down,
    )


def solution(mesh):
    wide = P(("dp", "fsdp"), None)
    thin = P(("dp", "fsdp"))
    seq = P("dp", "fsdp", None)
    group = P("dp", None)
    return jax.shard_map(
        device_step,
        mesh=mesh,
        in_specs=(seq, seq, group, group, thin, thin, wide, wide, thin, thin, wide, wide),
        out_specs=(seq, seq, thin, thin, wide, wide, thin, thin, wide, wide),
        check_vma=False,
    )
```

```python
import functools
import math

import jax
import jax.numpy as jnp
from jax import lax
from jax.experimental import pallas as pl
from jax.experimental.pallas import tpu as pltpu
from jax.sharding import PartitionSpec as P


DEPTH = 48
EPS = 1e-05
ROWS = 256
HALF = 128
GROUP = 3
BACK_GROUP = 2
BF = jnp.bfloat16
F32 = jnp.float32
ALPHA = 1.0 / math.sqrt(DEPTH)
GELU_C = 0.7978845608028654
GELU_A = 0.044715
VMEM_LIMIT = 60 * 1024 * 1024


def dot(a, b, ca=1, cb=0):
    return lax.dot_general(a, b, (((ca,), (cb,)), ((), ())), preferred_element_type=F32)


def norm(v):
    c = v - jnp.mean(v, axis=-1, keepdims=True)
    r = lax.rsqrt(jnp.mean(c * c, axis=-1, keepdims=True) + EPS)
    return c * r, r


def norm_back(f, n, r):
    return r * (f - jnp.mean(f, axis=-1, keepdims=True) - n * jnp.mean(f * n, axis=-1, keepdims=True))


def params(n):
    return pltpu.CompilerParams(
        dimension_semantics=("arbitrary",) * n, vmem_limit_bytes=VMEM_LIMIT
    )


def cost(micros, moved):
    return pl.CostEstimate(flops=int(micros * 1e9), transcendentals=0, bytes_accessed=moved)


def last_block(lens, m):
    return (lens[m] + (ROWS - 1)) // ROWS - 1


def attn_fwd_kernel(lens, x_ref, w_ref, vec_ref, qkv_ref, low_ref, lse_ref, kv_ref):
    m = pl.program_id(0)
    i = pl.program_id(1)
    d = x_ref.shape[2]
    live = i <= last_block(lens, m)

    @pl.when(live)
    def _():
        n, _ = norm(x_ref[0].astype(F32))
        low = (n * vec_ref[0:1, :] + vec_ref[1:2, :]).astype(BF)
        for t in range(3):
            part = dot(low, w_ref[:, t * d:(t + 1) * d]).astype(BF)
            qkv_ref[0, :, t * d:(t + 1) * d] = part
            if t:
                kv_ref[pl.ds(pl.multiple_of(i * ROWS, ROWS), ROWS), (t - 1) * d:t * d] = part

    part = lens[m] - i * ROWS <= HALF

    def variant(ii, size):
        keys = ii * ROWS + size

        @pl.when(live & (i == ii) & (part == (size == HALF)))
        def _():
            lane = lax.broadcasted_iota(jnp.int32, (size, 128), 1)
            row = lax.broadcasted_iota(jnp.int32, (size, size), 0)
            key = lax.broadcasted_iota(jnp.int32, (size, size), 1)
            allowed = (key <= row) & (key + ii * ROWS < lens[m])

            def group(gp, cols):
                spans, scores, values = [], [], []
                for sub in range(GROUP):
                    at = pl.multiple_of((gp * GROUP + sub) * 128, 128)
                    spans.append(pl.ds(at, 128))
                    q = qkv_ref[0, 0:size, pl.ds(at, 128)].astype(F32) * 0.125
                    k = kv_ref[0:keys, pl.ds(at, 128)]
                    values.append(kv_ref[0:keys, pl.ds(pl.multiple_of(d + at, 128), 128)])
                    for h in range(2):
                        qh = jnp.where((lane < 64) == (h == 0), q, 0.0).astype(BF)
                        scores.append(dot(qh, k, 1, 1))
                outs = []
                for n, s in enumerate(scores):
                    tail = jnp.where(allowed, s[:, ii * ROWS:], -1e30)
                    s = tail if ii == 0 else jnp.concatenate([s[:, :ii * ROWS], tail], axis=1)
                    peak = jnp.max(s, axis=-1, keepdims=True)
                    e = jnp.exp(s - peak)
                    total = jnp.sum(e, axis=-1, keepdims=True)
                    p = (e * (1.0 / total)).astype(BF)
                    outs.append(dot(p, values[n // 2]))
                    cols = jnp.where(lane == gp * (2 * GROUP) + n, peak + jnp.log(total), cols)
                for sub, span in enumerate(spans):
                    low_ref[0, 0:size, span] = jnp.where(lane < 64, outs[2 * sub], outs[2 * sub + 1]).astype(BF)
                return cols

            cols = lax.fori_loop(0, d // (128 * GROUP), group, jnp.zeros((size, 128), F32))
            lse_ref[0, :, 0:size] = jnp.transpose(cols)[0:16]

    for ii in range(x_rows_blocks(kv_ref)):
        variant(ii, ROWS)
        if ii:
            variant(ii, HALF)


def x_rows_blocks(ref):
    return ref.shape[0] // ROWS


def attn_fwd(lens, x, w, vec):
    mb, rows, d = x.shape
    nb = rows // ROWS

    def blk(m, i, ln):
        return (m, jnp.minimum(i, last_block(ln, m)), 0)

    return pl.pallas_call(
        attn_fwd_kernel,
        grid_spec=pltpu.PrefetchScalarGridSpec(
            num_scalar_prefetch=1,
            grid=(mb, nb),
            in_specs=[
                pl.BlockSpec((1, ROWS, d), blk),
                pl.BlockSpec((d, 3 * d), lambda m, i, ln: (0, 0), pipeline_mode=pl.Buffered(1)),
                pl.BlockSpec((8, d), lambda m, i, ln: (0, 0)),
            ],
            out_specs=[
                pl.BlockSpec((1, ROWS, 3 * d), blk),
                pl.BlockSpec((1, ROWS, d), blk),
                pl.BlockSpec((1, 16, ROWS), lambda m, i, ln: (m, 0, jnp.minimum(i, last_block(ln, m)))),
            ],
            scratch_shapes=[pltpu.VMEM((rows, 2 * d), BF)],
        ),
        out_shape=[
            jax.ShapeDtypeStruct((mb, rows, 3 * d), BF),
            jax.ShapeDtypeStruct((mb, rows, d), BF),
            jax.ShapeDtypeStruct((mb, 16, rows), F32),
        ],
        compiler_params=params(2),
        cost_estimate=cost(60, 20 << 20),
        name="attn_fwd",
    )(lens, x, w, vec)


def weight_copies(rest_ref, down_ref, wout_ref, wup_ref, wdown_ref, sem):
    d = wout_ref.shape[0]
    ff = wup_ref.shape[1]
    chunks = ff // d

    def out():
        return pltpu.make_async_copy(rest_ref.at[:, ff:ff + d], wout_ref, sem.at[2 * chunks])

    def up(c):
        at = pl.ds(pl.multiple_of(c * d, 128), d)
        return pltpu.make_async_copy(rest_ref.at[:, at], wup_ref.at[:, at], sem.at[c])

    def down(c):
        at = pl.ds(pl.multiple_of(c * d, 128), d)
        return pltpu.make_async_copy(down_ref.at[at, :], wdown_ref.at[at, :], sem.at[chunks + c])

    def start():
        out().start()
        for c in range(chunks):
            up(c).start()
            down(c).start()

    return start, out, up, down


def run_chunks(chunk, count, opening):
    if opening:
        lax.fori_loop(0, count, chunk, 0)
    else:
        for c in range(count):
            chunk(c, 0)


def mlp_fwd_kernel(lens, low_ref, x_ref, vec_ref, rest_ref, down_ref, out_ref, mid_ref,
                   wout_ref, wup_ref, wdown_ref, y_ref, sem):
    m = pl.program_id(0)
    i = pl.program_id(1)
    d = x_ref.shape[2]
    live = i <= last_block(lens, m)
    part = lens[m] - i * ROWS <= HALF
    first = (m == 0) & (i == 0)
    start, get_out, get_up, get_down = weight_copies(rest_ref, down_ref, wout_ref, wup_ref, wdown_ref, sem)

    @pl.when(first)
    def _():
        start()
        get_out().wait()

    @pl.when(jnp.logical_not(live))
    def _():
        out_ref[...] = jnp.zeros_like(out_ref)

    def body(size, opening):
        @pl.when(live & (part == (size == HALF)) & (first == opening))
        def _():
            alive = lax.broadcasted_iota(jnp.int32, (size, 1), 0) + i * ROWS < lens[m]
            middle = x_ref[0, 0:size].astype(F32) + ALPHA * dot(low_ref[0, 0:size], wout_ref[...])
            mid_ref[0, 0:size] = middle
            n2, _ = norm(middle)
            second = (n2 * vec_ref[2:3, :] + vec_ref[3:4, :]).astype(BF)
            y_ref[0:size] = jnp.zeros((size, d), F32)

            def chunk(c, carry):
                if opening:
                    get_up(c).wait()
                    get_down(c).wait()
                    at = pl.ds(pl.multiple_of(c * d, 128), d)
                else:
                    at = slice(c * d, (c + 1) * d)
                up = dot(second, wup_ref[:, at])
                t = jnp.tanh(GELU_C * (up + GELU_A * up * up * up))
                y_ref[0:size] += dot((up * (0.5 * (1.0 + t))).astype(BF), wdown_ref[at, :])
                return carry

            run_chunks(chunk, wup_ref.shape[1] // d, opening)
            out_ref[0, 0:size] = jnp.where(alive, middle + ALPHA * y_ref[0:size], 0.0).astype(BF)
            if size < ROWS:
                out_ref[0, size:] = jnp.zeros((ROWS - size, d), BF)

    body(ROWS, True)
    body(ROWS, False)
    body(HALF, False)


def mlp_fwd(lens, low, x, rest, wdown, vec):
    mb, rows, d = x.shape
    ff = wdown.shape[0]

    def blk(m, i, ln):
        return (m, jnp.minimum(i, last_block(ln, m)), 0)

    return pl.pallas_call(
        mlp_fwd_kernel,
        grid_spec=pltpu.PrefetchScalarGridSpec(
            num_scalar_prefetch=1,
            grid=(mb, rows // ROWS),
            in_specs=[
                pl.BlockSpec((1, ROWS, d), blk),
                pl.BlockSpec((1, ROWS, d), blk),
                pl.BlockSpec((8, d), lambda m, i, ln: (0, 0)),
                pl.BlockSpec(memory_space=pl.ANY),
                pl.BlockSpec(memory_space=pl.ANY),
            ],
            out_specs=[
                pl.BlockSpec((1, ROWS, d), lambda m, i, ln: (m, i, 0)),
                pl.BlockSpec((1, ROWS, d), blk),
            ],
            scratch_shapes=[
                pltpu.VMEM((d, d), BF),
                pltpu.VMEM((d, ff), BF),
                pltpu.VMEM((ff, d), BF),
                pltpu.VMEM((ROWS, d), F32),
                pltpu.SemaphoreType.DMA((2 * (ff // d) + 1,)),
            ],
        ),
        out_shape=[
            jax.ShapeDtypeStruct((mb, rows, d), BF),
            jax.ShapeDtypeStruct((mb, rows, d), F32),
        ],
        compiler_params=params(2),
        cost_estimate=cost(40, 40 << 20),
        name="mlp_fwd",
    )(lens, low, x, vec, rest, wdown)


def mlp_bwd_kernel(lens, core, low_ref, mid_ref, cot_ref, vec_ref, rest_ref, wd_ref,
                   gmid_ref, gmix_ref, inner_ref, keep_ref, give_ref, gdown_ref,
                   wout_ref, wup_ref, wdown_ref, aout_ref, aup_ref, adown_ref, gvec_ref, e2_ref,
                   stage_ref, down_ref, sem, half_sem, *, share):
    m = pl.program_id(0)
    i = pl.program_id(1)
    d = mid_ref.shape[2]
    ff = wup_ref.shape[1]
    chunks = ff // d
    live = i <= last_block(lens, m)
    part = lens[m] - i * ROWS <= HALF
    first = (m == 0) & (i == 0)
    final = (m == pl.num_programs(0) - 1) & (i == pl.num_programs(1) - 1)
    start, get_out, get_up, get_down = weight_copies(rest_ref, wd_ref, wout_ref, wup_ref, wdown_ref, sem)

    @pl.when(first)
    def _():
        start()
        aout_ref[...] = jnp.zeros_like(aout_ref)
        aup_ref[...] = jnp.zeros_like(aup_ref)
        adown_ref[...] = jnp.zeros_like(adown_ref)
        gvec_ref[...] = jnp.zeros_like(gvec_ref)
        get_out().wait()

    def body(size):
        @pl.when(live & (part == (size == HALF)))
        def _():
            alive = lax.broadcasted_iota(jnp.int32, (size, 1), 0) + i * ROWS < lens[m]
            low = low_ref[0, 0:size]
            n2, r2 = norm(mid_ref[0, 0:size])
            gain = vec_ref[2:3, :]
            second = (n2 * gain + vec_ref[3:4, :]).astype(BF)
            second_t = jnp.transpose(second)
            gout = jnp.where(alive, cot_ref[0, 0:size].astype(F32), 0.0)
            gmlp = (ALPHA * gout).astype(BF)
            e2_ref[0:size] = jnp.zeros((size, d), F32)

            def chunk(c, carry):
                @pl.when(first)
                def _():
                    get_up(c).wait()
                    get_down(c).wait()

                at = pl.ds(pl.multiple_of(c * d, 128), d)
                up = dot(second, wup_ref[:, at])
                back = dot(gmlp, wdown_ref[at, :], 1, 1)
                sq = up * up
                t = jnp.tanh(GELU_C * (up + GELU_A * sq * up))
                half = 0.5 * (1.0 + t)
                act = (up * half).astype(BF)
                slope = half + 0.5 * up * (1.0 - t * t) * (GELU_C * (1.0 + 3.0 * GELU_A * sq))
                gup = (back * slope).astype(BF)
                adown_ref[at, :] += dot(act, gmlp, 0, 0)
                e2_ref[0:size] += dot(gup, wup_ref[:, at], 1, 1)
                aup_ref[:, at] += dot(second_t, gup)
                return carry

            lax.fori_loop(0, chunks, chunk, 0)
            e2 = e2_ref[0:size]
            gvec_ref[0:1, :] += jnp.sum(e2 * n2, axis=0, keepdims=True)
            gvec_ref[1:2, :] += jnp.sum(e2, axis=0, keepdims=True)
            gmid = gout + norm_back(e2 * gain, n2, r2)
            gmid_ref[0, 0:size] = gmid
            gao = (ALPHA * gmid).astype(BF)
            gmix = dot(gao, wout_ref[...], 1, 1).astype(BF)
            aout_ref[...] += dot(low, gao, 0, 0)
            gmix_ref[0, 0:size] = gmix
            prod = gmix.astype(F32) * low.astype(F32)
            head = lax.broadcasted_iota(jnp.int32, (16, d), 0)
            lane = lax.broadcasted_iota(jnp.int32, (16, d), 1)
            pick = jnp.where(lane // 64 == head, 1.0, 0.0).astype(F32)
            inner_ref[0, :, 0:size] = lax.dot_general(
                pick, prod, (((1,), (1,)), ((), ())),
                preferred_element_type=F32, precision=lax.Precision.HIGHEST,
            )

    body(ROWS)
    body(HALF)

    @pl.when(final)
    def _():
        main = d + ff
        stage_ref[:, 0:d] = aout_ref[...].astype(BF)
        stage_ref[:, d:main] = aup_ref[...].astype(BF)
        each = keep_ref.shape[1]

        def halves(step):
            for n in range(2 * keep_ref.shape[0]):
                src = stage_ref.at[n * each:(n + 1) * each, :]

                @pl.when(core[0] == n % 2)
                def _():
                    step(pltpu.make_async_copy(src, keep_ref.at[n // 2], half_sem.at[n]))

                @pl.when(core[0] != n % 2)
                def _():
                    step(pltpu.make_async_copy(src, give_ref.at[n // 2], half_sem.at[n]))

        halves(lambda c: c.start())
        if share % 8 == 0:

            def regroup(e, carry):
                for c in range(chunks):
                    at = 2 * chunks * share * e + c * share
                    one = adown_ref[pl.ds(pl.multiple_of(at, 8), share), :]
                    two = adown_ref[pl.ds(pl.multiple_of(at + chunks * share, 8), share), :]
                    both = jnp.concatenate([one, two], axis=0).astype(BF)
                    down_ref[pl.ds(pl.multiple_of(2 * share * e, 16), 2 * share), c * d:(c + 1) * d] = both
                return carry

            lax.fori_loop(0, d // (2 * share), regroup, 0)
        else:
            for c in range(chunks):
                down_ref[:, c * d:(c + 1) * d] = adown_ref[c * d:(c + 1) * d, :].astype(BF)
        down_ref[:, ff:ff + 128] = jnp.transpose(gvec_ref[...]).astype(BF)
        last = pltpu.make_async_copy(down_ref, gdown_ref, sem.at[1])
        last.start()
        halves(lambda c: c.wait())
        last.wait()


def mlp_bwd(lens, core, low, mid, cot, rest, wdown, vec, share, dp):
    mb, rows, d = mid.shape
    ff = wdown.shape[0]

    def blk(m, i, ln, core):
        return (m, jnp.minimum(i, last_block(ln, m)), 0)

    return pl.pallas_call(
        functools.partial(mlp_bwd_kernel, share=share),
        grid_spec=pltpu.PrefetchScalarGridSpec(
            num_scalar_prefetch=2,
            grid=(mb, rows // ROWS),
            in_specs=[
                pl.BlockSpec((1, ROWS, d), blk),
                pl.BlockSpec((1, ROWS, d), blk),
                pl.BlockSpec((1, ROWS, d), blk),
                pl.BlockSpec((8, d), lambda m, i, ln, core: (0, 0)),
                pl.BlockSpec(memory_space=pl.ANY),
                pl.BlockSpec(memory_space=pl.ANY),
            ],
            out_specs=[
                pl.BlockSpec((1, ROWS, d), blk),
                pl.BlockSpec((1, ROWS, d), blk),
                pl.BlockSpec((1, 16, ROWS), lambda m, i, ln, core: (m, 0, jnp.minimum(i, last_block(ln, m)))),
                pl.BlockSpec(memory_space=pl.ANY),
                pl.BlockSpec(memory_space=pl.ANY),
                pl.BlockSpec(memory_space=pl.ANY),
            ],
            scratch_shapes=[
                pltpu.VMEM((d, d), BF),
                pltpu.VMEM((d, ff), BF),
                pltpu.VMEM((ff, d), BF),
                pltpu.VMEM((d, d), F32),
                pltpu.VMEM((d, ff), F32),
                pltpu.VMEM((ff, d), F32),
                pltpu.VMEM((128, d), F32),
                pltpu.VMEM((ROWS, d), F32),
                pltpu.VMEM((d, d + ff), BF),
                pltpu.VMEM((d, ff + 128), BF),
                pltpu.SemaphoreType.DMA((2 * (ff // d) + 1,)),
                pltpu.SemaphoreType.DMA((dp,)),
            ],
        ),
        out_shape=[
            jax.ShapeDtypeStruct((mb, rows, d), F32),
            jax.ShapeDtypeStruct((mb, rows, d), BF),
            jax.ShapeDtypeStruct((mb, 16, rows), F32),
            jax.ShapeDtypeStruct((dp // 2, d // dp, d + ff), BF),
            jax.ShapeDtypeStruct((dp // 2, d // dp, d + ff), BF),
            jax.ShapeDtypeStruct((d, ff + 128), BF),
        ],
        compiler_params=params(2),
        cost_estimate=cost(80, 60 << 20),
        name="mlp_bwd",
    )(lens, core, low, mid, cot, vec, rest, wdown)


def attn_bwd_kernel(lens, core, x_ref, q_ref, k_ref, v_ref, gmix_ref, gmid_ref, lse_ref, inner_ref,
                    w_ref, vec_ref, *rest, m, begin):
    if begin:
        dx_ref, gw_ref, acc_ref, gvec_ref, dk_ref, dv_ref, gq_ref = rest
    else:
        prev_ref, dx_ref, keep_ref, give_ref, acc_ref, gvec_ref, dk_ref, dv_ref, gq_ref, before_ref, sem = rest
    g = pl.program_id(0)
    i = pl.num_programs(0) - 1 - g
    d = x_ref.shape[2]
    end = last_block(lens, m)
    live = i <= end

    @pl.when(g == 0)
    def _():
        if not begin:
            pltpu.make_async_copy(prev_ref, before_ref, sem).start()
        acc_ref[...] = jnp.zeros_like(acc_ref)
        gvec_ref[...] = jnp.zeros_like(gvec_ref)

    @pl.when(jnp.logical_not(live))
    def _():
        dx_ref[...] = jnp.zeros_like(dx_ref)

    part = lens[m] - i * ROWS <= HALF

    def variant(ii, size):
        keys = ii * ROWS + size

        @pl.when(live & (i == ii) & (part == (size == HALF)))
        def _():
            lane = lax.broadcasted_iota(jnp.int32, (size, 128), 1)
            key = lax.broadcasted_iota(jnp.int32, (size, size), 0)
            row = lax.broadcasted_iota(jnp.int32, (size, size), 1)
            allowed = (key <= row) & (key + ii * ROWS < lens[m])
            fresh = end == ii

            def group(gp, carry):
                spans, keep = [], []
                for sub in range(BACK_GROUP):
                    hp = gp * BACK_GROUP + sub
                    span = pl.ds(pl.multiple_of(hp * 128, 128), 128)
                    spans.append(span)
                    q = q_ref[0, 0:size, span].astype(F32) * 0.125
                    gm = gmix_ref[0, 0:size, span]
                    k = k_ref[0, 0:keys, span]
                    v = v_ref[0, 0:keys, span]
                    for h in range(2):
                        mine = (lane < 64) == (h == 0)
                        qh = jnp.where(mine, q, 0.0).astype(BF)
                        gh = jnp.where(mine, gm, jnp.zeros_like(gm))
                        keep.append((hp * 2 + h, qh, gh, dot(k, qh, 1, 1), dot(v, gh, 1, 1)))
                results = []
                for sub in range(BACK_GROUP):
                    k_t = jnp.transpose(k_ref[0, 0:keys, spans[sub]])
                    probs, grads, dqs = [], [], []
                    for h in range(2):
                        head, _, _, s, dp = keep[2 * sub + h]
                        tail = jnp.where(allowed, s[ii * ROWS:], -1e30)
                        s = tail if ii == 0 else jnp.concatenate([s[:ii * ROWS], tail], axis=0)
                        p = jnp.exp(s - lse_ref[0, pl.ds(head, 1), :][:, 0:size])
                        ds = (p * (dp - inner_ref[0, pl.ds(head, 1), :][:, 0:size])).astype(BF)
                        dqs.append(dot(k_t, ds)[h * 64:(h + 1) * 64])
                        probs.append(p.astype(BF))
                        grads.append(ds)
                    both = keep[2 * sub:2 * sub + 2]
                    dv = dot(jnp.concatenate(probs, axis=1), jnp.concatenate([b[2] for b in both], axis=0))
                    dk = dot(jnp.concatenate(grads, axis=1), jnp.concatenate([b[1] for b in both], axis=0))
                    dq = jnp.transpose(jnp.concatenate(dqs, axis=0)) * 0.125
                    results.append((dq, dk, dv))
                for span, (dq, dk, dv) in zip(spans, results):
                    gq_ref[0:size, span] = dq.astype(BF)
                    dv_ref[0:keys, span] = jnp.where(fresh, 0.0, dv_ref[0:keys, span]) + dv
                    dk_ref[0:keys, span] = jnp.where(fresh, 0.0, dk_ref[0:keys, span]) + dk
                return carry

            lax.fori_loop(0, d // (128 * BACK_GROUP), group, 0)

    for ii in range(x_rows_blocks(dk_ref)):
        variant(ii, ROWS)
        if ii:
            variant(ii, HALF)

    def finish(size):
        @pl.when(live & (part == (size == HALF)))
        def _():
            base = pl.ds(pl.multiple_of(i * ROWS, ROWS), size)
            gq_ref[0:size, d:2 * d] = dk_ref[base, :].astype(BF)
            gq_ref[0:size, 2 * d:] = dv_ref[base, :].astype(BF)
            n1, r1 = norm(x_ref[0, 0:size].astype(F32))
            gain = vec_ref[0:1, :]
            low_t = jnp.transpose((n1 * gain + vec_ref[1:2, :]).astype(BF))
            e1 = jnp.zeros((size, d), F32)
            for t in range(3):
                at = slice(t * d, (t + 1) * d)
                gq = gq_ref[0:size, at]
                e1 = e1 + dot(gq, w_ref[:, at], 1, 1)
                acc_ref[:, at] += dot(low_t, gq)
            gvec_ref[0:1, :] += jnp.sum(e1 * n1, axis=0, keepdims=True)
            gvec_ref[1:2, :] += jnp.sum(e1, axis=0, keepdims=True)
            alive = lax.broadcasted_iota(jnp.int32, (size, 1), 0) + i * ROWS < lens[m]
            dx = gmid_ref[0, 0:size] + norm_back(e1 * gain, n1, r1)
            dx_ref[0, 0:size] = jnp.where(alive, dx, 0.0).astype(BF)
            if size < ROWS:
                dx_ref[0, size:] = jnp.zeros((ROWS - size, d), BF)

    finish(ROWS)
    finish(HALF)

    @pl.when(i == 0)
    def _():
        rows = jnp.transpose(gvec_ref[...])
        if begin:
            gw_ref[:, 0:3 * d] = acc_ref[...].astype(BF)
            gw_ref[:, 3 * d:] = rows.astype(BF)
        else:
            pltpu.make_async_copy(prev_ref, before_ref, sem).wait()
            each = keep_ref.shape[1]
            for n in range(2 * keep_ref.shape[0]):
                at = slice(n * each, (n + 1) * each)
                wide = (acc_ref[at, :] + before_ref[at, 0:3 * d].astype(F32)).astype(BF)
                thin = (rows[at] + before_ref[at, 3 * d:].astype(F32)).astype(BF)

                @pl.when(core[0] == n % 2)
                def _():
                    keep_ref[n // 2, :, 0:3 * d] = wide
                    keep_ref[n // 2, :, 3 * d:] = thin

                @pl.when(core[0] != n % 2)
                def _():
                    give_ref[n // 2, :, 0:3 * d] = wide
                    give_ref[n // 2, :, 3 * d:] = thin


def attn_bwd(m, prev, dp, lens, core, x, qkv, gmix, gmid, lse, inner, gathered, vec):
    _, rows, d = x.shape
    nb = rows // ROWS
    begin = m == 0

    def blk(g, ln, core):
        return (m, jnp.minimum(nb - 1 - g, last_block(ln, m)), 0)

    def stat(g, ln, core):
        return (m, 0, jnp.minimum(nb - 1 - g, last_block(ln, m)))

    def fixed(g, ln, core):
        return (0, 0)

    one = pl.Buffered(1)
    whole = (d, 3 * d)
    wide = (d, 3 * d + 128)
    split = (dp // 2, d // dp, 3 * d + 128)
    return pl.pallas_call(
        functools.partial(attn_bwd_kernel, m=m, begin=begin),
        grid_spec=pltpu.PrefetchScalarGridSpec(
            num_scalar_prefetch=2,
            grid=(nb,),
            in_specs=[
                pl.BlockSpec((1, ROWS, d), blk),
                pl.BlockSpec((1, ROWS, d), blk),
                pl.BlockSpec((1, rows, d), lambda g, ln, core: (m, 0, 1), pipeline_mode=one),
                pl.BlockSpec((1, rows, d), lambda g, ln, core: (m, 0, 2), pipeline_mode=one),
                pl.BlockSpec((1, ROWS, d), blk),
                pl.BlockSpec((1, ROWS, d), blk),
                pl.BlockSpec((1, 16, ROWS), stat),
                pl.BlockSpec((1, 16, ROWS), stat),
                pl.BlockSpec(whole, fixed, pipeline_mode=one),
                pl.BlockSpec((8, d), fixed),
            ] + ([] if begin else [pl.BlockSpec(memory_space=pl.ANY)]),
            out_specs=[
                pl.BlockSpec((1, ROWS, d), lambda g, ln, core: (0, nb - 1 - g, 0)),
            ] + ([pl.BlockSpec(wide, fixed, pipeline_mode=one)] if begin else [
                pl.BlockSpec(split, lambda g, ln, core: (0, 0, 0), pipeline_mode=one)] * 2),
            scratch_shapes=[
                pltpu.VMEM(whole, F32),
                pltpu.VMEM((128, d), F32),
                pltpu.VMEM((rows, d), F32),
                pltpu.VMEM((rows, d), F32),
                pltpu.VMEM((ROWS, 3 * d), BF),
            ] + ([] if begin else [pltpu.VMEM(wide, BF), pltpu.SemaphoreType.DMA(())]),
        ),
        out_shape=[jax.ShapeDtypeStruct((1, rows, d), BF)]
        + ([jax.ShapeDtypeStruct(wide, BF)] if begin else [jax.ShapeDtypeStruct(split, BF)] * 2),
        compiler_params=params(1),
        cost_estimate=cost(40, 20 << 20),
        name="attn_bwd",
    )(lens, core, x, qkv, qkv, qkv, gmix, gmid, lse, inner, gathered, vec, *prev)


def place_blocks(table, pieces, blocks):
    each, rows, d = pieces[0].shape
    count = len(pieces)

    def kernel(at, *refs):
        srcs, out, held, sem = refs[:count], refs[count], refs[count + 1], refs[count + 2]
        slots = [(p, j, p * each + j) for p in range(count) for j in range(each)]
        loads = [pltpu.make_async_copy(srcs[p].at[j], held.at[k], sem.at[0, k]) for p, j, k in slots]
        stores = [pltpu.make_async_copy(held.at[k], out.at[at[k]], sem.at[1, k]) for p, j, k in slots]
        for c in loads:
            c.start()
        for load, store in zip(loads, stores):
            load.wait()
            store.start()
        for c in stores:
            c.wait()

    anywhere = pl.BlockSpec(memory_space=pl.ANY)
    return pl.pallas_call(
        kernel,
        grid_spec=pltpu.PrefetchScalarGridSpec(
            num_scalar_prefetch=1,
            grid=(1,),
            in_specs=[anywhere] * count,
            out_specs=anywhere,
            scratch_shapes=[
                pltpu.VMEM((count * each, rows, d), pieces[0].dtype),
                pltpu.SemaphoreType.DMA((2, count * each)),
            ],
        ),
        out_shape=jax.ShapeDtypeStruct((blocks, rows, d), pieces[0].dtype),
        compiler_params=params(1),
        cost_estimate=cost(4, 2 * blocks * rows * d * 2),
        name="place_blocks",
    )(table, *pieces)


def place_weights(table, sides, main, d):
    count, share, width = sides[0].shape
    chunks = (width - main) // d
    total = 2 * count * share

    def kernel(at, *refs):
        srcs, out, rest = refs[:2], refs[2], refs[3:]
        held, sem = rest[-2:]

        def load(side, k):
            return pltpu.make_async_copy(srcs[side].at[k], held.at[side, k], sem.at[side, k, chunks + 1])

        def stores(side, k):
            to = at[side * count + k]
            src = held.at[side, k]
            row = pl.ds(pl.multiple_of(to * share, 8), share)
            every = [pltpu.make_async_copy(src.at[:, 0:main], out.at[row, :], sem.at[side, k, 0])]
            for c in range(chunks):
                row = pl.ds(pl.multiple_of((to * chunks + c) * share, 8), share)
                col = slice(main + c * d, main + (c + 1) * d)
                every.append(pltpu.make_async_copy(src.at[:, col], rest[0].at[row, :], sem.at[side, k, c + 1]))
            return every

        for side in range(2):
            def begin(k, carry, side=side):
                load(side, k).start()
                return carry

            lax.fori_loop(0, count, begin, 0)
        for side in range(2):
            def turn(k, carry, side=side):
                load(side, k).wait()
                for c in stores(side, k):
                    c.start()
                return carry

            lax.fori_loop(0, count, turn, 0)
        for side in range(2):
            def end(k, carry, side=side):
                for c in stores(side, k):
                    c.wait()
                return carry

            lax.fori_loop(0, count, end, 0)

    anywhere = pl.BlockSpec(memory_space=pl.ANY)
    shapes = [jax.ShapeDtypeStruct((total, main), BF)]
    if chunks:
        shapes.append(jax.ShapeDtypeStruct((total * chunks, d), BF))
    return pl.pallas_call(
        kernel,
        grid_spec=pltpu.PrefetchScalarGridSpec(
            num_scalar_prefetch=1,
            grid=(1,),
            in_specs=[anywhere] * 2,
            out_specs=[anywhere] * len(shapes),
            scratch_shapes=[
                pltpu.VMEM((2, count, share, width), BF),
                pltpu.SemaphoreType.DMA((2, count, chunks + 2)),
            ],
        ),
        out_shape=shapes,
        compiler_params=params(1),
        cost_estimate=cost(8, 2 * total * width * 2),
        name="place_weights",
    )(table, *sides)


def swap(x, axis, bits):
    size = lax.axis_size(axis)
    return lax.ppermute(x, axis, [(s, s ^ bits) for s in range(size)])


def exchange(parts, axis):
    size = lax.axis_size(axis)
    return [parts[0]] + [swap(parts[b], axis, b) for b in range(1, size)]


def staged_gather(shard, main, d):
    dp = lax.axis_size("dp")
    zs = lax.axis_size("fsdp")
    chips = dp // 2
    got = jnp.stack(exchange([shard] * zs, "fsdp"))
    got = jnp.stack([got] + [swap(got, "dp", 2 * b) for b in range(1, chips)])
    share, width = shard.shape
    mine = got.reshape(chips * zs, share, width)
    other = swap(mine, "dp", 1)
    place = lax.axis_index("dp")
    z = lax.axis_index("fsdp")
    at = lax.iota(jnp.int32, chips * zs)
    table = jnp.concatenate([
        (place ^ (2 * (at // zs) + core)) * zs + (z ^ (at % zs)) for core in range(2)
    ])
    if share % 8 == 0:
        return place_weights(table, (mine, other), main, d)
    order = jnp.zeros_like(table).at[table].set(lax.iota(jnp.int32, dp * zs))
    whole = jnp.take(jnp.concatenate([mine, other]), order, axis=0, mode="clip")
    parts = [whole[:, :, :main].reshape(-1, main)]
    if width > main:
        down = whole[:, :, main:].reshape(dp * zs, share, -1, d).transpose(0, 2, 1, 3)
        parts.append(down.reshape(-1, d))
    return parts


def sum_plane(mine, other):
    chip = lax.axis_index("dp") // 2

    def part(b):
        pick = [lax.dynamic_index_in_dim(t, chip ^ b, 0, keepdims=False) for t in (mine, other)]
        return (pick[0].astype(F32) + pick[1].astype(F32)).astype(BF)

    count = mine.shape[0]
    return [part(0)] + [swap(part(b), "dp", 2 * b) for b in range(1, count)]


def total_of(parts):
    acc = parts[0].astype(F32)
    for p in parts[1:]:
        acc = acc + p.astype(F32)
    return acc


def sum_line(parts):
    zs = lax.axis_size("fsdp")
    z = lax.axis_index("fsdp")
    low = total_of(parts).astype(BF)
    low = low.reshape(zs, -1, low.shape[1])
    pieces = [lax.dynamic_index_in_dim(low, z ^ b, 0, keepdims=False) for b in range(zs)]
    return total_of(exchange(pieces, "fsdp"))


def device_step(tokens, cotangent, lengths, perm, ln1_gain, ln1_bias, w_qkv, w_out,
               ln2_gain, ln2_bias, w_up, w_down):
    zs = lax.axis_size("fsdp")
    dp = lax.axis_size("dp")
    devices = dp * zs
    core = (lax.axis_index("dp") % 2).reshape(1).astype(jnp.int32)
    z = lax.axis_index("fsdp")
    slots, rows, d = tokens.shape
    mb = slots // zs
    ff = w_up.shape[1]
    share = w_qkv.shape[0]
    chunks = ff // d
    dealing = perm[0]
    lens = lax.dynamic_slice_in_dim(lengths[0], z * mb, mb)
    order = (z ^ lax.iota(jnp.int32, zs))
    take_at = (order[:, None] * mb + lax.iota(jnp.int32, mb)[None, :]).reshape(-1)
    send_at = jnp.take(dealing, take_at, mode="clip")

    vectors = jnp.stack([ln1_gain, ln1_bias, ln2_gain, ln2_bias], axis=1)
    vectors = jnp.pad(vectors, ((0, 0), (0, 124)))
    down = w_down.reshape(chunks, share, d).transpose(1, 0, 2).reshape(share, ff)
    shard = jnp.concatenate([w_up, w_out, down], axis=1)
    (gathered,) = staged_gather(jnp.concatenate([w_qkv, vectors], axis=1), 3 * d + 128, d)
    rest, wdown = staged_gather(shard, ff + d, d)
    at = 3 * d
    vec = jnp.pad(jnp.transpose(gathered[:, at:at + 4]).astype(F32), ((0, 4), (0, 0)))

    def deal(array):
        parts = [jnp.take(array, send_at[b * mb:(b + 1) * mb], axis=0, mode="clip") for b in range(zs)]
        table = (lax.iota(jnp.int32, mb)[None, :] * zs + order[:, None]).reshape(-1)
        return place_blocks(table, exchange(parts, "fsdp"), slots).reshape(mb, zs * rows, d)

    def give_back(array):
        split = array.reshape(array.shape[0], zs, rows, d)
        parts = [lax.dynamic_index_in_dim(split, z ^ b, 1, keepdims=False) for b in range(zs)]
        return exchange(parts, "fsdp")

    x = deal(tokens)
    cot = deal(cotangent)
    qkv, low, lse = attn_fwd(lens, x, gathered, vec)
    out, mid = mlp_fwd(lens, low, x, rest, wdown, vec)
    cot, out = lax.optimization_barrier((cot, out))
    gmid, gmix, inner, keep, give, gdown = mlp_bwd(lens, core, low, mid, cot, rest, wdown, vec, share, dp)
    if share % 8:
        gtop = gdown[:, :ff].reshape(d, chunks, d).transpose(1, 0, 2)
        gtop = gtop.reshape(devices, chunks, share, d).transpose(0, 2, 1, 3).reshape(d, ff)
        gdown = jnp.concatenate([gtop, gdown[:, ff:]], axis=1)
    early = lax.psum_scatter(gdown, ("dp", "fsdp"), scatter_dimension=0, tiled=True)
    halves = (keep, swap(give, "dp", 1))
    planes = sum_plane(*halves)
    outs = give_back(out)
    grads = []
    prev = ()
    for m in range(mb):
        dx, *gw = attn_bwd(m, prev, dp, lens, core, x, qkv, gmix, gmid, lse, inner, gathered, vec)
        prev = tuple(gw)
        grads += give_back(dx)
        if m == 0:
            main = sum_line(planes)
    halves = (gw[0], swap(gw[1], "dp", 1))
    late = sum_plane(*halves)
    late = sum_line(late)
    block_out = place_blocks(send_at, outs, slots)
    d_tokens = place_blocks(send_at.reshape(zs, mb).T.reshape(-1), grads, slots)
    early = early.astype(F32)
    g_down = early[:, :ff].reshape(share, chunks, d).transpose(1, 0, 2).reshape(share * chunks, d)
    return (
        block_out,
        d_tokens,
        late[:, 3 * d],
        late[:, 3 * d + 1],
        late[:, :3 * d],
        main[:, :d],
        early[:, ff],
        early[:, ff + 1],
        main[:, d:],
        g_down,
    )


def solution(mesh):
    wide = P(("dp", "fsdp"), None)
    thin = P(("dp", "fsdp"))
    seq = P("dp", "fsdp", None)
    group = P("dp", None)
    return jax.shard_map(
        device_step,
        mesh=mesh,
        in_specs=(seq, seq, group, group, thin, thin, wide, wide, thin, thin, wide, wide),
        out_specs=(seq, seq, thin, thin, wide, wide, thin, thin, wide, wide),
        check_vma=False,
    )
```

```python
import functools
import math

import jax
import jax.numpy as jnp
from jax import lax
from jax.experimental import pallas as pl
from jax.experimental.pallas import tpu as pltpu
from jax.sharding import PartitionSpec as P


DEPTH = 48
EPS = 1e-05
ROWS = 256
HALF = 128
GROUP = 3
BACK_GROUP = 2
BF = jnp.bfloat16
F32 = jnp.float32
ALPHA = 1.0 / math.sqrt(DEPTH)
GELU_C = 0.7978845608028654
GELU_A = 0.044715
VMEM_LIMIT = 60 * 1024 * 1024


def dot(a, b, ca=1, cb=0):
    return lax.dot_general(a, b, (((ca,), (cb,)), ((), ())), preferred_element_type=F32)


def norm(v):
    c = v - jnp.mean(v, axis=-1, keepdims=True)
    r = lax.rsqrt(jnp.mean(c * c, axis=-1, keepdims=True) + EPS)
    return c * r, r


def norm_back(f, n, r):
    return r * (f - jnp.mean(f, axis=-1, keepdims=True) - n * jnp.mean(f * n, axis=-1, keepdims=True))


def params(n):
    return pltpu.CompilerParams(
        dimension_semantics=("arbitrary",) * n, vmem_limit_bytes=VMEM_LIMIT
    )


def cost(micros, moved):
    return pl.CostEstimate(flops=int(micros * 1e9), transcendentals=0, bytes_accessed=moved)


def last_block(lens, m):
    return (lens[m] + (ROWS - 1)) // ROWS - 1


def attn_fwd_kernel(lens, x_ref, w_ref, vec_ref, qkv_ref, low_ref, lse_ref, kv_ref):
    m = pl.program_id(0)
    i = pl.program_id(1)
    d = x_ref.shape[2]
    live = i <= last_block(lens, m)

    @pl.when(live)
    def _():
        n, _ = norm(x_ref[0].astype(F32))
        low = (n * vec_ref[0:1, :] + vec_ref[1:2, :]).astype(BF)
        for t in range(3):
            part = dot(low, w_ref[:, t * d:(t + 1) * d]).astype(BF)
            qkv_ref[0, :, t * d:(t + 1) * d] = part
            if t:
                kv_ref[pl.ds(pl.multiple_of(i * ROWS, ROWS), ROWS), (t - 1) * d:t * d] = part

    part = lens[m] - i * ROWS <= HALF

    def variant(ii, size):
        keys = ii * ROWS + size

        @pl.when(live & (i == ii) & (part == (size == HALF)))
        def _():
            lane = lax.broadcasted_iota(jnp.int32, (size, 128), 1)
            row = lax.broadcasted_iota(jnp.int32, (size, size), 0)
            key = lax.broadcasted_iota(jnp.int32, (size, size), 1)
            allowed = (key <= row) & (key + ii * ROWS < lens[m])

            def group(gp, cols):
                spans, scores, values = [], [], []
                for sub in range(GROUP):
                    at = pl.multiple_of((gp * GROUP + sub) * 128, 128)
                    spans.append(pl.ds(at, 128))
                    q = qkv_ref[0, 0:size, pl.ds(at, 128)].astype(F32) * 0.125
                    k = kv_ref[0:keys, pl.ds(at, 128)]
                    values.append(kv_ref[0:keys, pl.ds(pl.multiple_of(d + at, 128), 128)])
                    for h in range(2):
                        qh = jnp.where((lane < 64) == (h == 0), q, 0.0).astype(BF)
                        scores.append(dot(qh, k, 1, 1))
                outs = []
                for n, s in enumerate(scores):
                    tail = jnp.where(allowed, s[:, ii * ROWS:], -1e30)
                    s = tail if ii == 0 else jnp.concatenate([s[:, :ii * ROWS], tail], axis=1)
                    peak = jnp.max(s, axis=-1, keepdims=True)
                    e = jnp.exp(s - peak)
                    total = jnp.sum(e, axis=-1, keepdims=True)
                    p = (e * (1.0 / total)).astype(BF)
                    outs.append(dot(p, values[n // 2]))
                    cols = jnp.where(lane == gp * (2 * GROUP) + n, peak + jnp.log(total), cols)
                for sub, span in enumerate(spans):
                    low_ref[0, 0:size, span] = jnp.where(lane < 64, outs[2 * sub], outs[2 * sub + 1]).astype(BF)
                return cols

            cols = lax.fori_loop(0, d // (128 * GROUP), group, jnp.zeros((size, 128), F32))
            lse_ref[0, :, 0:size] = jnp.transpose(cols)[0:16]

    for ii in range(x_rows_blocks(kv_ref)):
        variant(ii, ROWS)
        if ii:
            variant(ii, HALF)


def x_rows_blocks(ref):
    return ref.shape[0] // ROWS


def attn_fwd(lens, x, w, vec):
    mb, rows, d = x.shape
    nb = rows // ROWS

    def blk(m, i, ln):
        return (m, jnp.minimum(i, last_block(ln, m)), 0)

    return pl.pallas_call(
        attn_fwd_kernel,
        grid_spec=pltpu.PrefetchScalarGridSpec(
            num_scalar_prefetch=1,
            grid=(mb, nb),
            in_specs=[
                pl.BlockSpec((1, ROWS, d), blk),
                pl.BlockSpec((d, 3 * d), lambda m, i, ln: (0, 0), pipeline_mode=pl.Buffered(1)),
                pl.BlockSpec((8, d), lambda m, i, ln: (0, 0)),
            ],
            out_specs=[
                pl.BlockSpec((1, ROWS, 3 * d), blk),
                pl.BlockSpec((1, ROWS, d), blk),
                pl.BlockSpec((1, 16, ROWS), lambda m, i, ln: (m, 0, jnp.minimum(i, last_block(ln, m)))),
            ],
            scratch_shapes=[pltpu.VMEM((rows, 2 * d), BF)],
        ),
        out_shape=[
            jax.ShapeDtypeStruct((mb, rows, 3 * d), BF),
            jax.ShapeDtypeStruct((mb, rows, d), BF),
            jax.ShapeDtypeStruct((mb, 16, rows), F32),
        ],
        compiler_params=params(2),
        cost_estimate=cost(60, 20 << 20),
        name="attn_fwd",
    )(lens, x, w, vec)


def weight_copies(rest_ref, down_ref, wout_ref, wup_ref, wdown_ref, sem):
    d = wout_ref.shape[0]
    ff = wup_ref.shape[1]
    chunks = ff // d

    def out():
        return pltpu.make_async_copy(rest_ref.at[:, ff:ff + d], wout_ref, sem.at[2 * chunks])

    def up(c):
        at = pl.ds(pl.multiple_of(c * d, 128), d)
        return pltpu.make_async_copy(rest_ref.at[:, at], wup_ref.at[:, at], sem.at[c])

    def down(c):
        at = pl.ds(pl.multiple_of(c * d, 128), d)
        return pltpu.make_async_copy(down_ref.at[at, :], wdown_ref.at[at, :], sem.at[chunks + c])

    def start():
        out().start()
        for c in range(chunks):
            up(c).start()
            down(c).start()

    return start, out, up, down


def run_chunks(chunk, count, opening):
    if opening:
        lax.fori_loop(0, count, chunk, 0)
    else:
        for c in range(count):
            chunk(c, 0)


def mlp_fwd_kernel(lens, low_ref, x_ref, vec_ref, rest_ref, down_ref, out_ref, mid_ref,
                   wout_ref, wup_ref, wdown_ref, y_ref, sem):
    m = pl.program_id(0)
    i = pl.program_id(1)
    d = x_ref.shape[2]
    live = i <= last_block(lens, m)
    part = lens[m] - i * ROWS <= HALF
    first = (m == 0) & (i == 0)
    start, get_out, get_up, get_down = weight_copies(rest_ref, down_ref, wout_ref, wup_ref, wdown_ref, sem)

    @pl.when(first)
    def _():
        start()
        get_out().wait()

    @pl.when(jnp.logical_not(live))
    def _():
        out_ref[...] = jnp.zeros_like(out_ref)

    def body(size, opening):
        @pl.when(live & (part == (size == HALF)) & (first == opening))
        def _():
            alive = lax.broadcasted_iota(jnp.int32, (size, 1), 0) + i * ROWS < lens[m]
            middle = x_ref[0, 0:size].astype(F32) + ALPHA * dot(low_ref[0, 0:size], wout_ref[...])
            mid_ref[0, 0:size] = middle
            n2, _ = norm(middle)
            second = (n2 * vec_ref[2:3, :] + vec_ref[3:4, :]).astype(BF)
            y_ref[0:size] = jnp.zeros((size, d), F32)

            def chunk(c, carry):
                if opening:
                    get_up(c).wait()
                    get_down(c).wait()
                    at = pl.ds(pl.multiple_of(c * d, 128), d)
                else:
                    at = slice(c * d, (c + 1) * d)
                up = dot(second, wup_ref[:, at])
                t = jnp.tanh(GELU_C * (up + GELU_A * up * up * up))
                y_ref[0:size] += dot((up * (0.5 * (1.0 + t))).astype(BF), wdown_ref[at, :])
                return carry

            run_chunks(chunk, wup_ref.shape[1] // d, opening)
            out_ref[0, 0:size] = jnp.where(alive, middle + ALPHA * y_ref[0:size], 0.0).astype(BF)
            if size < ROWS:
                out_ref[0, size:] = jnp.zeros((ROWS - size, d), BF)

    body(ROWS, True)
    body(ROWS, False)
    body(HALF, False)


def mlp_fwd(lens, low, x, rest, wdown, vec):
    mb, rows, d = x.shape
    ff = wdown.shape[0]

    def blk(m, i, ln):
        return (m, jnp.minimum(i, last_block(ln, m)), 0)

    return pl.pallas_call(
        mlp_fwd_kernel,
        grid_spec=pltpu.PrefetchScalarGridSpec(
            num_scalar_prefetch=1,
            grid=(mb, rows // ROWS),
            in_specs=[
                pl.BlockSpec((1, ROWS, d), blk),
                pl.BlockSpec((1, ROWS, d), blk),
                pl.BlockSpec((8, d), lambda m, i, ln: (0, 0)),
                pl.BlockSpec(memory_space=pl.ANY),
                pl.BlockSpec(memory_space=pl.ANY),
            ],
            out_specs=[
                pl.BlockSpec((1, ROWS, d), lambda m, i, ln: (m, i, 0)),
                pl.BlockSpec((1, ROWS, d), blk),
            ],
            scratch_shapes=[
                pltpu.VMEM((d, d), BF),
                pltpu.VMEM((d, ff), BF),
                pltpu.VMEM((ff, d), BF),
                pltpu.VMEM((ROWS, d), F32),
                pltpu.SemaphoreType.DMA((2 * (ff // d) + 1,)),
            ],
        ),
        out_shape=[
            jax.ShapeDtypeStruct((mb, rows, d), BF),
            jax.ShapeDtypeStruct((mb, rows, d), F32),
        ],
        compiler_params=params(2),
        cost_estimate=cost(40, 40 << 20),
        name="mlp_fwd",
    )(lens, low, x, vec, rest, wdown)


def mlp_bwd_kernel(lens, core, low_ref, mid_ref, cot_ref, vec_ref, rest_ref, wd_ref,
                   gmid_ref, gmix_ref, inner_ref, keep_ref, give_ref, gdown_ref,
                   wout_ref, wup_ref, wdown_ref, aout_ref, aup_ref, adown_ref, gvec_ref, e2_ref,
                   stage_ref, down_ref, sem, half_sem, down_sem, *, share):
    m = pl.program_id(0)
    i = pl.program_id(1)
    d = mid_ref.shape[2]
    ff = wup_ref.shape[1]
    chunks = ff // d
    live = i <= last_block(lens, m)
    part = lens[m] - i * ROWS <= HALF
    first = (m == 0) & (i == 0)
    final = (m == pl.num_programs(0) - 1) & (i == pl.num_programs(1) - 1)
    start, get_out, get_up, get_down = weight_copies(rest_ref, wd_ref, wout_ref, wup_ref, wdown_ref, sem)

    @pl.when(first)
    def _():
        start()
        aout_ref[...] = jnp.zeros_like(aout_ref)
        aup_ref[...] = jnp.zeros_like(aup_ref)
        adown_ref[...] = jnp.zeros_like(adown_ref)
        gvec_ref[...] = jnp.zeros_like(gvec_ref)
        get_out().wait()

    def body(size):
        @pl.when(live & (part == (size == HALF)))
        def _():
            alive = lax.broadcasted_iota(jnp.int32, (size, 1), 0) + i * ROWS < lens[m]
            low = low_ref[0, 0:size]
            n2, r2 = norm(mid_ref[0, 0:size])
            gain = vec_ref[2:3, :]
            second = (n2 * gain + vec_ref[3:4, :]).astype(BF)
            second_t = jnp.transpose(second)
            gout = jnp.where(alive, cot_ref[0, 0:size].astype(F32), 0.0)
            gmlp = (ALPHA * gout).astype(BF)
            e2_ref[0:size] = jnp.zeros((size, d), F32)

            def chunk(c, carry):
                @pl.when(first)
                def _():
                    get_up(c).wait()
                    get_down(c).wait()

                at = pl.ds(pl.multiple_of(c * d, 128), d)
                up = dot(second, wup_ref[:, at])
                back = dot(gmlp, wdown_ref[at, :], 1, 1)
                sq = up * up
                t = jnp.tanh(GELU_C * (up + GELU_A * sq * up))
                half = 0.5 * (1.0 + t)
                act = (up * half).astype(BF)
                slope = half + 0.5 * up * (1.0 - t * t) * (GELU_C * (1.0 + 3.0 * GELU_A * sq))
                gup = (back * slope).astype(BF)
                adown_ref[at, :] += dot(act, gmlp, 0, 0)
                e2_ref[0:size] += dot(gup, wup_ref[:, at], 1, 1)
                aup_ref[:, at] += dot(second_t, gup)
                return carry

            lax.fori_loop(0, chunks, chunk, 0)
            e2 = e2_ref[0:size]
            gvec_ref[0:1, :] += jnp.sum(e2 * n2, axis=0, keepdims=True)
            gvec_ref[1:2, :] += jnp.sum(e2, axis=0, keepdims=True)
            gmid = gout + norm_back(e2 * gain, n2, r2)
            gmid_ref[0, 0:size] = gmid
            gao = (ALPHA * gmid).astype(BF)
            gmix = dot(gao, wout_ref[...], 1, 1).astype(BF)
            aout_ref[...] += dot(low, gao, 0, 0)
            gmix_ref[0, 0:size] = gmix
            prod = gmix.astype(F32) * low.astype(F32)
            head = lax.broadcasted_iota(jnp.int32, (16, d), 0)
            lane = lax.broadcasted_iota(jnp.int32, (16, d), 1)
            pick = jnp.where(lane // 64 == head, 1.0, 0.0).astype(F32)
            inner_ref[0, :, 0:size] = lax.dot_general(
                pick, prod, (((1,), (1,)), ((), ())),
                preferred_element_type=F32, precision=lax.Precision.HIGHEST,
            )

    body(ROWS)
    body(HALF)

    @pl.when(final)
    def _():
        each = keep_ref.shape[1]

        def halves(step, ready):
            for n in range(2 * keep_ref.shape[0]):
                at = slice(n * each, (n + 1) * each)
                ready(at)
                src = stage_ref.at[at, :]

                @pl.when(core[0] == n % 2)
                def _():
                    step(pltpu.make_async_copy(src, keep_ref.at[n // 2], half_sem.at[n]))

                @pl.when(core[0] != n % 2)
                def _():
                    step(pltpu.make_async_copy(src, give_ref.at[n // 2], half_sem.at[n]))

        def lower(at):
            stage_ref[at, 0:d] = aout_ref[at, :].astype(BF)
            stage_ref[at, d:] = aup_ref[at, :].astype(BF)

        halves(lambda c: c.start(), lower)
        down_ref[:, ff:ff + 128] = jnp.transpose(gvec_ref[...]).astype(BF)
        if share % 8 == 0:
            pair = 2 * share

            def leave(e):
                at = pl.ds(pl.multiple_of(pair * e, 16), pair)
                return pltpu.make_async_copy(down_ref.at[at, :], gdown_ref.at[at, :], down_sem.at[e])

            def regroup(e, carry):
                for c in range(chunks):
                    at = chunks * pair * e + c * share
                    one = adown_ref[pl.ds(pl.multiple_of(at, 8), share), :]
                    two = adown_ref[pl.ds(pl.multiple_of(at + chunks * share, 8), share), :]
                    both = jnp.concatenate([one, two], axis=0).astype(BF)
                    down_ref[pl.ds(pl.multiple_of(pair * e, 16), pair), c * d:(c + 1) * d] = both
                leave(e).start()
                return carry

            def settle(e, carry):
                leave(e).wait()
                return carry

            lax.fori_loop(0, d // pair, regroup, 0)
            halves(lambda c: c.wait(), lambda at: None)
            lax.fori_loop(0, d // pair, settle, 0)
        else:
            for c in range(chunks):
                down_ref[:, c * d:(c + 1) * d] = adown_ref[c * d:(c + 1) * d, :].astype(BF)
            last = pltpu.make_async_copy(down_ref, gdown_ref, down_sem.at[0])
            last.start()
            halves(lambda c: c.wait(), lambda at: None)
            last.wait()


def mlp_bwd(lens, core, low, mid, cot, rest, wdown, vec, share, dp):
    mb, rows, d = mid.shape
    ff = wdown.shape[0]

    def blk(m, i, ln, core):
        return (m, jnp.minimum(i, last_block(ln, m)), 0)

    return pl.pallas_call(
        functools.partial(mlp_bwd_kernel, share=share),
        grid_spec=pltpu.PrefetchScalarGridSpec(
            num_scalar_prefetch=2,
            grid=(mb, rows // ROWS),
            in_specs=[
                pl.BlockSpec((1, ROWS, d), blk),
                pl.BlockSpec((1, ROWS, d), blk),
                pl.BlockSpec((1, ROWS, d), blk),
                pl.BlockSpec((8, d), lambda m, i, ln, core: (0, 0)),
                pl.BlockSpec(memory_space=pl.ANY),
                pl.BlockSpec(memory_space=pl.ANY),
            ],
            out_specs=[
                pl.BlockSpec((1, ROWS, d), blk),
                pl.BlockSpec((1, ROWS, d), blk),
                pl.BlockSpec((1, 16, ROWS), lambda m, i, ln, core: (m, 0, jnp.minimum(i, last_block(ln, m)))),
                pl.BlockSpec(memory_space=pl.ANY),
                pl.BlockSpec(memory_space=pl.ANY),
                pl.BlockSpec(memory_space=pl.ANY),
            ],
            scratch_shapes=[
                pltpu.VMEM((d, d), BF),
                pltpu.VMEM((d, ff), BF),
                pltpu.VMEM((ff, d), BF),
                pltpu.VMEM((d, d), F32),
                pltpu.VMEM((d, ff), F32),
                pltpu.VMEM((ff, d), F32),
                pltpu.VMEM((128, d), F32),
                pltpu.VMEM((ROWS, d), F32),
                pltpu.VMEM((d, d + ff), BF),
                pltpu.VMEM((d, ff + 128), BF),
                pltpu.SemaphoreType.DMA((2 * (ff // d) + 1,)),
                pltpu.SemaphoreType.DMA((dp,)),
                pltpu.SemaphoreType.DMA((max(1, d // (2 * share)),)),
            ],
        ),
        out_shape=[
            jax.ShapeDtypeStruct((mb, rows, d), F32),
            jax.ShapeDtypeStruct((mb, rows, d), BF),
            jax.ShapeDtypeStruct((mb, 16, rows), F32),
            jax.ShapeDtypeStruct((dp // 2, d // dp, d + ff), BF),
            jax.ShapeDtypeStruct((dp // 2, d // dp, d + ff), BF),
            jax.ShapeDtypeStruct((d, ff + 128), BF),
        ],
        compiler_params=params(2),
        cost_estimate=cost(80, 60 << 20),
        name="mlp_bwd",
    )(lens, core, low, mid, cot, vec, rest, wdown)


def attn_bwd_kernel(lens, core, x_ref, q_ref, k_ref, v_ref, gmix_ref, gmid_ref, lse_ref, inner_ref,
                    w_hbm, vec_ref, *rest, m, begin):
    *rest, w_ref, w_sem = rest
    w_copy = pltpu.make_async_copy(w_hbm.at[:, 0:w_ref.shape[1]], w_ref, w_sem)
    if begin:
        dx_ref, gw_ref, acc_ref, gvec_ref, dk_ref, dv_ref, gq_ref = rest
    else:
        prev_ref, dx_ref, keep_ref, give_ref, acc_ref, gvec_ref, dk_ref, dv_ref, gq_ref, before_ref, sem = rest
    g = pl.program_id(0)
    i = pl.num_programs(0) - 1 - g
    d = x_ref.shape[2]
    end = last_block(lens, m)
    live = i <= end

    @pl.when(g == 0)
    def _():
        w_copy.start()
        if not begin:
            pltpu.make_async_copy(prev_ref, before_ref, sem).start()
        acc_ref[...] = jnp.zeros_like(acc_ref)
        gvec_ref[...] = jnp.zeros_like(gvec_ref)

    @pl.when(jnp.logical_not(live))
    def _():
        dx_ref[...] = jnp.zeros_like(dx_ref)

    part = lens[m] - i * ROWS <= HALF

    def variant(ii, size):
        keys = ii * ROWS + size

        @pl.when(live & (i == ii) & (part == (size == HALF)))
        def _():
            lane = lax.broadcasted_iota(jnp.int32, (size, 128), 1)
            key = lax.broadcasted_iota(jnp.int32, (size, size), 0)
            row = lax.broadcasted_iota(jnp.int32, (size, size), 1)
            allowed = (key <= row) & (key + ii * ROWS < lens[m])
            fresh = end == ii

            def group(gp, carry):
                spans, keep = [], []
                for sub in range(BACK_GROUP):
                    hp = gp * BACK_GROUP + sub
                    span = pl.ds(pl.multiple_of(hp * 128, 128), 128)
                    spans.append(span)
                    q = q_ref[0, 0:size, span].astype(F32) * 0.125
                    gm = gmix_ref[0, 0:size, span]
                    k = k_ref[0, 0:keys, span]
                    v = v_ref[0, 0:keys, span]
                    for h in range(2):
                        mine = (lane < 64) == (h == 0)
                        qh = jnp.where(mine, q, 0.0).astype(BF)
                        gh = jnp.where(mine, gm, jnp.zeros_like(gm))
                        keep.append((hp * 2 + h, qh, gh, dot(k, qh, 1, 1), dot(v, gh, 1, 1)))
                results = []
                for sub in range(BACK_GROUP):
                    k_t = jnp.transpose(k_ref[0, 0:keys, spans[sub]])
                    probs, grads, dqs = [], [], []
                    for h in range(2):
                        head, _, _, s, dp = keep[2 * sub + h]
                        tail = jnp.where(allowed, s[ii * ROWS:], -1e30)
                        s = tail if ii == 0 else jnp.concatenate([s[:ii * ROWS], tail], axis=0)
                        p = jnp.exp(s - lse_ref[0, pl.ds(head, 1), :][:, 0:size])
                        ds = (p * (dp - inner_ref[0, pl.ds(head, 1), :][:, 0:size])).astype(BF)
                        dqs.append(dot(k_t, ds)[h * 64:(h + 1) * 64])
                        probs.append(p.astype(BF))
                        grads.append(ds)
                    both = keep[2 * sub:2 * sub + 2]
                    dv = dot(jnp.concatenate(probs, axis=1), jnp.concatenate([b[2] for b in both], axis=0))
                    dk = dot(jnp.concatenate(grads, axis=1), jnp.concatenate([b[1] for b in both], axis=0))
                    dq = jnp.transpose(jnp.concatenate(dqs, axis=0)) * 0.125
                    results.append((dq, dk, dv))
                for span, (dq, dk, dv) in zip(spans, results):
                    gq_ref[0:size, span] = dq.astype(BF)
                    dv_ref[0:keys, span] = jnp.where(fresh, 0.0, dv_ref[0:keys, span]) + dv
                    dk_ref[0:keys, span] = jnp.where(fresh, 0.0, dk_ref[0:keys, span]) + dk
                return carry

            lax.fori_loop(0, d // (128 * BACK_GROUP), group, 0)

    for ii in range(x_rows_blocks(dk_ref)):
        variant(ii, ROWS)
        if ii:
            variant(ii, HALF)

    @pl.when(i == end)
    def _():
        w_copy.wait()

    def finish(size):
        @pl.when(live & (part == (size == HALF)))
        def _():
            base = pl.ds(pl.multiple_of(i * ROWS, ROWS), size)
            gq_ref[0:size, d:2 * d] = dk_ref[base, :].astype(BF)
            gq_ref[0:size, 2 * d:] = dv_ref[base, :].astype(BF)
            n1, r1 = norm(x_ref[0, 0:size].astype(F32))
            gain = vec_ref[0:1, :]
            low_t = jnp.transpose((n1 * gain + vec_ref[1:2, :]).astype(BF))
            e1 = jnp.zeros((size, d), F32)
            for t in range(3):
                at = slice(t * d, (t + 1) * d)
                gq = gq_ref[0:size, at]
                e1 = e1 + dot(gq, w_ref[:, at], 1, 1)
                acc_ref[:, at] += dot(low_t, gq)
            gvec_ref[0:1, :] += jnp.sum(e1 * n1, axis=0, keepdims=True)
            gvec_ref[1:2, :] += jnp.sum(e1, axis=0, keepdims=True)
            alive = lax.broadcasted_iota(jnp.int32, (size, 1), 0) + i * ROWS < lens[m]
            dx = gmid_ref[0, 0:size] + norm_back(e1 * gain, n1, r1)
            dx_ref[0, 0:size] = jnp.where(alive, dx, 0.0).astype(BF)
            if size < ROWS:
                dx_ref[0, size:] = jnp.zeros((ROWS - size, d), BF)

    finish(ROWS)
    finish(HALF)

    @pl.when(i == 0)
    def _():
        rows = jnp.transpose(gvec_ref[...])
        if begin:
            gw_ref[:, 0:3 * d] = acc_ref[...].astype(BF)
            gw_ref[:, 3 * d:] = rows.astype(BF)
        else:
            pltpu.make_async_copy(prev_ref, before_ref, sem).wait()
            each = keep_ref.shape[1]
            for n in range(2 * keep_ref.shape[0]):
                at = slice(n * each, (n + 1) * each)
                wide = (acc_ref[at, :] + before_ref[at, 0:3 * d].astype(F32)).astype(BF)
                thin = (rows[at] + before_ref[at, 3 * d:].astype(F32)).astype(BF)

                @pl.when(core[0] == n % 2)
                def _():
                    keep_ref[n // 2, :, 0:3 * d] = wide
                    keep_ref[n // 2, :, 3 * d:] = thin

                @pl.when(core[0] != n % 2)
                def _():
                    give_ref[n // 2, :, 0:3 * d] = wide
                    give_ref[n // 2, :, 3 * d:] = thin


def attn_bwd(m, prev, dp, lens, core, x, qkv, gmix, gmid, lse, inner, gathered, vec):
    _, rows, d = x.shape
    nb = rows // ROWS
    begin = m == 0

    def blk(g, ln, core):
        return (m, jnp.minimum(nb - 1 - g, last_block(ln, m)), 0)

    def stat(g, ln, core):
        return (m, 0, jnp.minimum(nb - 1 - g, last_block(ln, m)))

    def fixed(g, ln, core):
        return (0, 0)

    one = pl.Buffered(1)
    whole = (d, 3 * d)
    wide = (d, 3 * d + 128)
    split = (dp // 2, d // dp, 3 * d + 128)
    return pl.pallas_call(
        functools.partial(attn_bwd_kernel, m=m, begin=begin),
        grid_spec=pltpu.PrefetchScalarGridSpec(
            num_scalar_prefetch=2,
            grid=(nb,),
            in_specs=[
                pl.BlockSpec((1, ROWS, d), blk),
                pl.BlockSpec((1, ROWS, d), blk),
                pl.BlockSpec((1, rows, d), lambda g, ln, core: (m, 0, 1), pipeline_mode=one),
                pl.BlockSpec((1, rows, d), lambda g, ln, core: (m, 0, 2), pipeline_mode=one),
                pl.BlockSpec((1, ROWS, d), blk),
                pl.BlockSpec((1, ROWS, d), blk),
                pl.BlockSpec((1, 16, ROWS), stat),
                pl.BlockSpec((1, 16, ROWS), stat),
                pl.BlockSpec(memory_space=pl.ANY),
                pl.BlockSpec((8, d), fixed),
            ] + ([] if begin else [pl.BlockSpec(memory_space=pl.ANY)]),
            out_specs=[
                pl.BlockSpec((1, ROWS, d), lambda g, ln, core: (0, nb - 1 - g, 0)),
            ] + ([pl.BlockSpec(wide, fixed, pipeline_mode=one)] if begin else [
                pl.BlockSpec(split, lambda g, ln, core: (0, 0, 0), pipeline_mode=one)] * 2),
            scratch_shapes=[
                pltpu.VMEM(whole, F32),
                pltpu.VMEM((128, d), F32),
                pltpu.VMEM((rows, d), F32),
                pltpu.VMEM((rows, d), F32),
                pltpu.VMEM((ROWS, 3 * d), BF),
            ] + ([] if begin else [pltpu.VMEM(wide, BF), pltpu.SemaphoreType.DMA(())])
            + [pltpu.VMEM(whole, BF), pltpu.SemaphoreType.DMA(())],
        ),
        out_shape=[jax.ShapeDtypeStruct((1, rows, d), BF)]
        + ([jax.ShapeDtypeStruct(wide, BF)] if begin else [jax.ShapeDtypeStruct(split, BF)] * 2),
        compiler_params=params(1),
        cost_estimate=cost(40, 20 << 20),
        name="attn_bwd",
    )(lens, core, x, qkv, qkv, qkv, gmix, gmid, lse, inner, gathered, vec, *prev)


def place_blocks(table, pieces, blocks):
    each, rows, d = pieces[0].shape
    count = len(pieces)

    def kernel(at, *refs):
        srcs, out, held, sem = refs[:count], refs[count], refs[count + 1], refs[count + 2]
        slots = [(p, j, p * each + j) for p in range(count) for j in range(each)]
        loads = [pltpu.make_async_copy(srcs[p].at[j], held.at[k], sem.at[0, k]) for p, j, k in slots]
        stores = [pltpu.make_async_copy(held.at[k], out.at[at[k]], sem.at[1, k]) for p, j, k in slots]
        for c in loads:
            c.start()
        for load, store in zip(loads, stores):
            load.wait()
            store.start()
        for c in stores:
            c.wait()

    anywhere = pl.BlockSpec(memory_space=pl.ANY)
    return pl.pallas_call(
        kernel,
        grid_spec=pltpu.PrefetchScalarGridSpec(
            num_scalar_prefetch=1,
            grid=(1,),
            in_specs=[anywhere] * count,
            out_specs=anywhere,
            scratch_shapes=[
                pltpu.VMEM((count * each, rows, d), pieces[0].dtype),
                pltpu.SemaphoreType.DMA((2, count * each)),
            ],
        ),
        out_shape=jax.ShapeDtypeStruct((blocks, rows, d), pieces[0].dtype),
        compiler_params=params(1),
        cost_estimate=cost(4, 2 * blocks * rows * d * 2),
        name="place_blocks",
    )(table, *pieces)


def place_weights(table, sides, main, d):
    count, share, width = sides[0].shape
    chunks = (width - main) // d
    total = 2 * count * share

    def kernel(at, *refs):
        srcs, out, rest = refs[:2], refs[2], refs[3:]
        held, sem = rest[-2:]

        def load(side, k):
            return pltpu.make_async_copy(srcs[side].at[k], held.at[side, k], sem.at[side, k, chunks + 1])

        def stores(side, k):
            to = at[side * count + k]
            src = held.at[side, k]
            row = pl.ds(pl.multiple_of(to * share, 8), share)
            every = [pltpu.make_async_copy(src.at[:, 0:main], out.at[row, :], sem.at[side, k, 0])]
            for c in range(chunks):
                row = pl.ds(pl.multiple_of((to * chunks + c) * share, 8), share)
                col = slice(main + c * d, main + (c + 1) * d)
                every.append(pltpu.make_async_copy(src.at[:, col], rest[0].at[row, :], sem.at[side, k, c + 1]))
            return every

        for side in range(2):
            def begin(k, carry, side=side):
                load(side, k).start()
                return carry

            lax.fori_loop(0, count, begin, 0)
        for side in range(2):
            def turn(k, carry, side=side):
                load(side, k).wait()
                for c in stores(side, k):
                    c.start()
                return carry

            lax.fori_loop(0, count, turn, 0)
        for side in range(2):
            def end(k, carry, side=side):
                for c in stores(side, k):
                    c.wait()
                return carry

            lax.fori_loop(0, count, end, 0)

    anywhere = pl.BlockSpec(memory_space=pl.ANY)
    shapes = [jax.ShapeDtypeStruct((total, main), BF)]
    if chunks:
        shapes.append(jax.ShapeDtypeStruct((total * chunks, d), BF))
    return pl.pallas_call(
        kernel,
        grid_spec=pltpu.PrefetchScalarGridSpec(
            num_scalar_prefetch=1,
            grid=(1,),
            in_specs=[anywhere] * 2,
            out_specs=[anywhere] * len(shapes),
            scratch_shapes=[
                pltpu.VMEM((2, count, share, width), BF),
                pltpu.SemaphoreType.DMA((2, count, chunks + 2)),
            ],
        ),
        out_shape=shapes,
        compiler_params=params(1),
        cost_estimate=cost(8, 2 * total * width * 2),
        name="place_weights",
    )(table, *sides)


def swap(x, axis, bits):
    size = lax.axis_size(axis)
    return lax.ppermute(x, axis, [(s, s ^ bits) for s in range(size)])


def exchange(parts, axis):
    size = lax.axis_size(axis)
    return [parts[0]] + [swap(parts[b], axis, b) for b in range(1, size)]


def staged_gather(shard, main, d):
    dp = lax.axis_size("dp")
    zs = lax.axis_size("fsdp")
    chips = dp // 2
    got = jnp.stack(exchange([shard] * zs, "fsdp"))
    got = jnp.stack([got] + [swap(got, "dp", 2 * b) for b in range(1, chips)])
    share, width = shard.shape
    mine = got.reshape(chips * zs, share, width)
    other = swap(mine, "dp", 1)
    place = lax.axis_index("dp")
    z = lax.axis_index("fsdp")
    at = lax.iota(jnp.int32, chips * zs)
    table = jnp.concatenate([
        (place ^ (2 * (at // zs) + core)) * zs + (z ^ (at % zs)) for core in range(2)
    ])
    if share % 8 == 0:
        return place_weights(table, (mine, other), main, d)
    order = jnp.zeros_like(table).at[table].set(lax.iota(jnp.int32, dp * zs))
    whole = jnp.take(jnp.concatenate([mine, other]), order, axis=0, mode="clip")
    parts = [whole[:, :, :main].reshape(-1, main)]
    if width > main:
        down = whole[:, :, main:].reshape(dp * zs, share, -1, d).transpose(0, 2, 1, 3)
        parts.append(down.reshape(-1, d))
    return parts


def sum_plane(mine, other):
    chip = lax.axis_index("dp") // 2

    def part(b):
        pick = [lax.dynamic_index_in_dim(t, chip ^ b, 0, keepdims=False) for t in (mine, other)]
        return (pick[0].astype(F32) + pick[1].astype(F32)).astype(BF)

    count = mine.shape[0]
    return [part(0)] + [swap(part(b), "dp", 2 * b) for b in range(1, count)]


def total_of(parts):
    acc = parts[0].astype(F32)
    for p in parts[1:]:
        acc = acc + p.astype(F32)
    return acc


def sum_line(parts):
    zs = lax.axis_size("fsdp")
    z = lax.axis_index("fsdp")
    low = total_of(parts).astype(BF)
    low = low.reshape(zs, -1, low.shape[1])
    pieces = [lax.dynamic_index_in_dim(low, z ^ b, 0, keepdims=False) for b in range(zs)]
    return total_of(exchange(pieces, "fsdp"))


def device_step(tokens, cotangent, lengths, perm, ln1_gain, ln1_bias, w_qkv, w_out,
               ln2_gain, ln2_bias, w_up, w_down):
    zs = lax.axis_size("fsdp")
    dp = lax.axis_size("dp")
    devices = dp * zs
    core = (lax.axis_index("dp") % 2).reshape(1).astype(jnp.int32)
    z = lax.axis_index("fsdp")
    slots, rows, d = tokens.shape
    mb = slots // zs
    ff = w_up.shape[1]
    share = w_qkv.shape[0]
    chunks = ff // d
    dealing = perm[0]
    lens = lax.dynamic_slice_in_dim(lengths[0], z * mb, mb)
    order = (z ^ lax.iota(jnp.int32, zs))
    take_at = (order[:, None] * mb + lax.iota(jnp.int32, mb)[None, :]).reshape(-1)
    send_at = jnp.take(dealing, take_at, mode="clip")

    vectors = jnp.stack([ln1_gain, ln1_bias, ln2_gain, ln2_bias], axis=1)
    vectors = jnp.pad(vectors, ((0, 0), (0, 124)))
    down = w_down.reshape(chunks, share, d).transpose(1, 0, 2).reshape(share, ff)
    shard = jnp.concatenate([w_up, w_out, down], axis=1)
    (gathered,) = staged_gather(jnp.concatenate([w_qkv, vectors], axis=1), 3 * d + 128, d)
    rest, wdown = staged_gather(shard, ff + d, d)
    at = 3 * d
    vec = jnp.pad(jnp.transpose(gathered[:, at:at + 4]).astype(F32), ((0, 4), (0, 0)))

    def deal(array):
        parts = [jnp.take(array, send_at[b * mb:(b + 1) * mb], axis=0, mode="clip") for b in range(zs)]
        table = (lax.iota(jnp.int32, mb)[None, :] * zs + order[:, None]).reshape(-1)
        return place_blocks(table, exchange(parts, "fsdp"), slots).reshape(mb, zs * rows, d)

    def give_back(array):
        split = array.reshape(array.shape[0], zs, rows, d)
        parts = [lax.dynamic_index_in_dim(split, z ^ b, 1, keepdims=False) for b in range(zs)]
        return exchange(parts, "fsdp")

    x = deal(tokens)
    cot = deal(cotangent)
    qkv, low, lse = attn_fwd(lens, x, gathered, vec)
    out, mid = mlp_fwd(lens, low, x, rest, wdown, vec)
    cot, out = lax.optimization_barrier((cot, out))
    gmid, gmix, inner, keep, give, gdown = mlp_bwd(lens, core, low, mid, cot, rest, wdown, vec, share, dp)
    if share % 8:
        gtop = gdown[:, :ff].reshape(d, chunks, d).transpose(1, 0, 2)
        gtop = gtop.reshape(devices, chunks, share, d).transpose(0, 2, 1, 3).reshape(d, ff)
        gdown = jnp.concatenate([gtop, gdown[:, ff:]], axis=1)
    early = lax.psum_scatter(gdown, ("dp", "fsdp"), scatter_dimension=0, tiled=True)
    halves = (keep, swap(give, "dp", 1))
    planes = sum_plane(*halves)
    outs = give_back(out)
    grads = []
    prev = ()
    for m in range(mb):
        dx, *gw = attn_bwd(m, prev, dp, lens, core, x, qkv, gmix, gmid, lse, inner, gathered, vec)
        prev = tuple(gw)
        grads += give_back(dx)
        if m == 0:
            main = sum_line(planes)
    halves = (gw[0], swap(gw[1], "dp", 1))
    late = sum_plane(*halves)
    late = sum_line(late)
    block_out = place_blocks(send_at, outs, slots)
    d_tokens = place_blocks(send_at.reshape(zs, mb).T.reshape(-1), grads, slots)
    early = early.astype(F32)
    g_down = early[:, :ff].reshape(share, chunks, d).transpose(1, 0, 2).reshape(share * chunks, d)
    return (
        block_out,
        d_tokens,
        late[:, 3 * d],
        late[:, 3 * d + 1],
        late[:, :3 * d],
        main[:, :d],
        early[:, ff],
        early[:, ff + 1],
        main[:, d:],
        g_down,
    )


def solution(mesh):
    wide = P(("dp", "fsdp"), None)
    thin = P(("dp", "fsdp"))
    seq = P("dp", "fsdp", None)
    group = P("dp", None)
    return jax.shard_map(
        device_step,
        mesh=mesh,
        in_specs=(seq, seq, group, group, thin, thin, wide, wide, thin, thin, wide, wide),
        out_specs=(seq, seq, thin, thin, wide, wide, thin, thin, wide, wide),
        check_vma=False,
    )
```
